32 devices in a mesh: row: 4 (over x, core), col: 8 (over z, y).
Axes of the slice: x: 2, y: 2, z: 4, core: 2. Of those that a mesh axis runs over, the one named last changes fastest.
Arguments:
- embeddings: bfloat16 [4096, 512], P(('row', 'col')), may hold values from -6 to 6
- sketch: bfloat16 [4096, 64], P(('row', 'col')), may hold values from -240 to 240
Outputs:
- basis: float32 [4096, 64], P(('row', 'col'))
- first_pass: float32 [4096, 64], P(('row', 'col'))
The draws below stay inside these ranges and needn't reach their ends.
All inputs are finite; a program needn't handle non-finite values.
Results may differ from the reference program's by a relative error of at most 0.00205.
Values may be sent and summed in bfloat16 or wider, within the bound.
No kernel may reach another device: no remote copies, remote signals or barrier semaphores. Data moves between devices by JAX's collectives and lax.ppermute only.
A program may use at most 64 MiB of HBM per device.

```python
import math
import jax
import jax.numpy as jnp
from jax import lax

D = 512
R = 64
NTOTAL = 4096


def draw_sketch(key, part):
    base = jnp.clip(jax.random.normal(key, (NTOTAL, R), jnp.float32), -6.0, 6.0)
    position = jnp.arange(NTOTAL, dtype=jnp.float32) / max(NTOTAL - 1, 1)
    scale = jnp.exp(math.log(3.0) * position)[:, None]
    return (base * scale).astype(jnp.bfloat16)


def level_of(rng, extent, shards, least, high):
    level, own = 1.0, jax.random.fold_in(rng, 6)
    for axis_at, blocks in shards:
        steps = jnp.exp(jax.random.uniform(jax.random.fold_in(own, axis_at), (blocks,), jnp.float32, least / len(shards), high / len(shards)))
        level = level * jnp.repeat(steps, extent[axis_at] // blocks).reshape([-1 if axis == axis_at else 1 for axis in range(len(extent))])
    return level


def scatter_about(rng, extent, scale, bound, pieces=(), held_as=jnp.bfloat16):
    values = jax.random.normal(rng, extent, jnp.float32) * scale
    if len(pieces) > 0:
        values = level_of(rng, extent, pieces, -0.22, 0.18) * values
    return jnp.clip(values, min=-bound, max=bound).astype(held_as)


def setup_inputs(seed: int = 0) -> dict:
    key_list = jax.random.split(jax.random.key(seed), 3)
    embeddings = scatter_about(key_list[0], (NTOTAL, D), 1.0, 6.0, ((0, 32),))
    sketch = draw_sketch(jax.random.fold_in(key_list[2], 71), 0)
    return {"embeddings": embeddings, "sketch": sketch}


def reference(embeddings, sketch):
    gamma = 3.0 / D
    norms = lax.optimization_barrier(jnp.sum(jnp.square(embeddings.astype(jnp.float32)), axis=1))
    size = 1024 if NTOTAL % 1024 == 0 else NTOTAL
    blocks = embeddings.reshape(NTOTAL // size, size, D)
    norm_blocks = norms.reshape(NTOTAL // size, size)

    def one_block(pair):
        rows, row_sq = pair
        cross = lax.dot_general(rows.astype(jnp.float32), embeddings.astype(jnp.float32), (((1,), (1,)), ((), ())), preferred_element_type=jnp.float32)
        dist = row_sq[:, None] + norms[None, :] - 2.0 * cross
        tile = jnp.exp(-gamma * dist).astype(jnp.bfloat16)
        return jnp.dot(tile.astype(jnp.float32), sketch.astype(jnp.float32), preferred_element_type=jnp.float32)
    sketched = lax.map(one_block, (blocks, norm_blocks)).reshape(NTOTAL, R)
    tests = sketch.astype(jnp.float32)
    core = jnp.dot(tests.T, sketched, precision=lax.Precision.HIGHEST)
    lower = jnp.linalg.cholesky(core)
    first = jax.scipy.linalg.solve_triangular(lower, sketched.T, lower=True).T
    gram_two = jnp.dot(first.T, first, precision=lax.Precision.HIGHEST)
    lower_two = jnp.linalg.cholesky(gram_two)
    second = jax.scipy.linalg.solve_triangular(lower_two, first.T, lower=True).T
    scale = jnp.sqrt(jnp.float32(NTOTAL))
    return (second * scale, first * scale)
```

```python
import functools

import jax
import jax.numpy as jnp
from jax import lax
from jax.experimental import pallas as pl
from jax.experimental.pallas import tpu as pltpu
from jax.sharding import PartitionSpec as P

AXES = ("row", "col")
HIGHEST = lax.Precision.HIGHEST
NT = (((1,), (1,)), ((), ()))
NN = (((1,), (0,)), ((), ()))
VMEM = pl.BlockSpec(memory_space=pltpu.VMEM)


def pack_kernel(points_ref, tests_ref, out_ref):
    count, width = points_ref.shape
    pieces = width // count
    depth = tests_ref.shape[0] // pieces
    out_ref[:count, :] = points_ref[...]
    for piece in range(pieces):
        out_ref[count:, piece * count : (piece + 1) * count] = tests_ref[
            piece * depth : (piece + 1) * depth, :
        ]


def tile_kernel(members, others, chunk, gamma, *refs):
    packs, refs = refs[: members + others - 1], refs[members + others - 1 :]
    total_ref, own_tests_ref, own, own_sq, facing, facing_tests = refs
    count = packs[0].shape[0] - own_tests_ref.shape[0] * own_tests_ref.shape[1] // (
        members * packs[0].shape[1]
    )
    pieces = packs[0].shape[1] // count
    depth = own_tests_ref.shape[0] // pieces

    def unpack(pack, points, tests, at):
        points[at * count : (at + 1) * count, :] = pack[:count, :]
        for piece in range(pieces):
            tests[piece * depth : (piece + 1) * depth, at * count : (at + 1) * count] = pack[
                count:, piece * count : (piece + 1) * count
            ]

    def squares(points):
        wide = points.astype(jnp.float32)
        return jnp.sum(wide * wide, axis=1, keepdims=True)

    for at in range(members):
        unpack(packs[at], own, own_tests_ref, at)
        column = squares(packs[at][:count, :])
        own_sq[:, at * count : (at + 1) * count] = jnp.broadcast_to(column, (count, count)).T[:8, :]
    for at in range(others):
        unpack(packs[0] if at == 0 else packs[members + at - 1], facing, facing_tests, at)
    total_ref[...] = jnp.zeros_like(total_ref)

    def step(index, carry):
        start = pl.multiple_of(index * chunk, chunk)
        block = facing[pl.ds(start, chunk), :]
        cross = lax.dot_general(block, own[...], NT, preferred_element_type=jnp.float32)
        dist = squares(block) + own_sq[:1, :] - 2.0 * cross
        tile = jnp.exp(-gamma * dist).astype(jnp.bfloat16)
        total_ref[...] += lax.dot_general(
            facing_tests[:, pl.ds(start, chunk)], tile, NN, preferred_element_type=jnp.float32
        )
        return carry

    lax.fori_loop(0, others * count // chunk, step, 0)


def tree(values):
    while len(values) > 1:
        values = [a + b for a, b in zip(values[::2], values[1::2])]
    return values[0]


def gram_kernel(members, *refs):
    totals, (tests_ref, gram_ref, sketched_ref) = refs[:members], refs[members:]
    count = sketched_ref.shape[1]
    grams = []
    for at in range(members):
        part = tree([
            totals[j][:, (at ^ j) * count : ((at ^ j) + 1) * count] for j in range(members)
        ])
        if at == 0:
            sketched_ref[...] = part
        both = jnp.concatenate(
            [tests_ref[:, at * count : (at + 1) * count].astype(jnp.float32), part], axis=0
        )
        grams.append(
            lax.dot_general(part, both, NT, precision=HIGHEST, preferred_element_type=jnp.float32)
        )
    gram_ref[...] = tree(grams)


def solve_kernel(scale, gram_ref, sketched_ref, basis_ref, first_ref):
    size = gram_ref.shape[0]
    rows = 8
    blocks = size // rows
    gram = gram_ref[...]
    core, inner = gram[:, :size], gram[:, size:]
    both = jnp.concatenate([(core + core.T) * 0.5, (inner + inner.T) * 0.5], axis=1)
    left = [both[rows * b : rows * (b + 1), :] for b in range(blocks)]
    outs = [[sketched_ref[rows * b : rows * (b + 1), :] for b in range(blocks)] for _ in range(2)]
    half = lax.broadcasted_iota(jnp.int32, (rows, 2 * size), 1) < size
    place = lax.broadcasted_iota(jnp.int32, (rows, 1), 0)
    wide = sketched_ref.shape[1]
    for k in range(size):
        at, inside = divmod(k, rows)
        line = left[at][inside : inside + 1, :]
        pivots = [line[:, k : k + 1], line[:, size + k : size + k + 1]]
        inverse = [1.0 / p for p in pivots]
        roots = [lax.rsqrt(p) for p in pivots]
        solved = [outs[s][at][inside : inside + 1, :] for s in range(2)]
        for b in range(at, blocks):
            factors = []
            for s in range(2):
                factor = left[b][:, s * size + k : s * size + k + 1] * inverse[s]
                if b == at:
                    factor = jnp.where(place > inside, factor, 0.0)
                factors.append(factor)
            for s in range(2):
                outs[s][b] = outs[s][b] - factors[s] * solved[s]
            left[b] = left[b] - jnp.where(
                half,
                jnp.broadcast_to(factors[0], (rows, 2 * size)),
                jnp.broadcast_to(factors[1], (rows, 2 * size)),
            ) * line
        first_ref[k : k + 1, :] = solved[0] * (roots[0] * scale)
        basis_ref[k : k + 1, :] = solved[1] * (roots[1] * scale)


def per_device(embeddings, sketch, rows, cols):
    count, width = embeddings.shape
    columns = sketch.shape[1]
    gamma = 3.0 / width
    near = 2 if cols % 2 == 0 else 1
    members, others = cols // near, rows * near
    devices = rows * cols

    def swap(value, mask):
        return lax.ppermute(value, AXES, [(i, i ^ mask) for i in range(devices)])

    tests = sketch.T
    packed_rows = count + columns * count // width
    packed = pl.pallas_call(
        pack_kernel,
        out_shape=jax.ShapeDtypeStruct((packed_rows, width), embeddings.dtype),
        in_specs=[VMEM, VMEM],
        out_specs=VMEM,
        name="pack",
    )(embeddings, tests)
    far_masks = [near * j for j in range(1, members)]
    side_masks = [2 * cols * x + l for x in range(rows // 2) for l in range(near)][1:]
    own = [packed] + [swap(packed, m) for m in far_masks]
    side = [packed] + [swap(packed, m) for m in side_masks]
    facing = side + [swap(b, cols) for b in side]
    wide = members * count
    total, own_tests = pl.pallas_call(
        functools.partial(tile_kernel, members, others, 256, gamma),
        out_shape=(
            jax.ShapeDtypeStruct((columns, wide), jnp.float32),
            jax.ShapeDtypeStruct((columns, wide), sketch.dtype),
        ),
        in_specs=[VMEM] * (members + others - 1),
        out_specs=(VMEM, VMEM),
        scratch_shapes=[
            pltpu.VMEM((wide, width), embeddings.dtype),
            pltpu.VMEM((8, wide), jnp.float32),
            pltpu.VMEM((others * count, width), embeddings.dtype),
            pltpu.VMEM((columns, others * count), sketch.dtype),
        ],
        name="tile",
    )(*own, *facing[1:])
    totals = [total] + [swap(total, m) for m in far_masks]
    gram, sketched = pl.pallas_call(
        functools.partial(gram_kernel, members),
        out_shape=(
            jax.ShapeDtypeStruct((columns, 2 * columns), jnp.float32),
            jax.ShapeDtypeStruct((columns, count), jnp.float32),
        ),
        in_specs=[VMEM] * (members + 1),
        out_specs=(VMEM, VMEM),
        name="gram",
    )(*totals, own_tests)
    mask = 1
    while mask < near:
        gram = gram + swap(gram, mask)
        mask *= 2
    mask = cols
    while mask < devices:
        gram = gram + swap(gram, mask)
        mask *= 2
    scale = float(devices * count) ** 0.5
    basis, first = pl.pallas_call(
        functools.partial(solve_kernel, scale),
        out_shape=(jax.ShapeDtypeStruct((columns, count), jnp.float32),) * 2,
        in_specs=[VMEM, VMEM],
        out_specs=(VMEM, VMEM),
        name="solve",
    )(gram, sketched)
    return basis.T, first.T


def solution(mesh):
    placed = P(AXES, None)
    return jax.shard_map(
        functools.partial(per_device, rows=mesh.shape["row"], cols=mesh.shape["col"]),
        mesh=mesh,
        in_specs=(placed, placed),
        out_specs=(placed, placed),
        check_vma=False,
    )
```

```python
import functools

import jax
import jax.numpy as jnp
from jax import lax
from jax.experimental import pallas as pl
from jax.experimental.pallas import tpu as pltpu
from jax.sharding import PartitionSpec as P

AXES = ("row", "col")
HIGHEST = lax.Precision.HIGHEST
NT = (((1,), (1,)), ((), ()))
NN = (((1,), (0,)), ((), ()))
VMEM = pl.BlockSpec(memory_space=pltpu.VMEM)


def pack_kernel(points_ref, tests_ref, out_ref):
    count, width = points_ref.shape
    pieces = width // count
    depth = tests_ref.shape[0] // pieces
    out_ref[:count, :] = points_ref[...]
    for piece in range(pieces):
        out_ref[count:, piece * count : (piece + 1) * count] = tests_ref[
            piece * depth : (piece + 1) * depth, :
        ]


def tile_kernel(members, others, chunk, gamma, *refs):
    packs, refs = refs[: members + others - 1], refs[members + others - 1 :]
    total_ref, own_tests_ref, own, own_sq, facing, facing_tests = refs
    count = packs[0].shape[0] - own_tests_ref.shape[0] * own_tests_ref.shape[1] // (
        members * packs[0].shape[1]
    )
    pieces = packs[0].shape[1] // count
    depth = own_tests_ref.shape[0] // pieces

    def unpack(pack, points, tests, at):
        points[at * count : (at + 1) * count, :] = pack[:count, :]
        for piece in range(pieces):
            tests[piece * depth : (piece + 1) * depth, at * count : (at + 1) * count] = pack[
                count:, piece * count : (piece + 1) * count
            ]

    def squares(points):
        wide = points.astype(jnp.float32)
        return jnp.sum(wide * wide, axis=1, keepdims=True)

    for at in range(members):
        unpack(packs[at], own, own_tests_ref, at)
        column = squares(packs[at][:count, :])
        own_sq[:, at * count : (at + 1) * count] = jnp.broadcast_to(column, (count, count)).T[:8, :]
    for at in range(others):
        unpack(packs[0] if at == 0 else packs[members + at - 1], facing, facing_tests, at)
    total_ref[...] = jnp.zeros_like(total_ref)

    def step(index, carry):
        start = pl.multiple_of(index * chunk, chunk)
        block = facing[pl.ds(start, chunk), :]
        cross = lax.dot_general(block, own[...], NT, preferred_element_type=jnp.float32)
        dist = squares(block) + own_sq[:1, :] - 2.0 * cross
        tile = jnp.exp(-gamma * dist).astype(jnp.bfloat16)
        total_ref[...] += lax.dot_general(
            facing_tests[:, pl.ds(start, chunk)], tile, NN, preferred_element_type=jnp.float32
        )
        return carry

    lax.fori_loop(0, others * count // chunk, step, 0)


def tree(values):
    while len(values) > 1:
        values = [a + b for a, b in zip(values[::2], values[1::2])]
    return values[0]


def gram_kernel(members, *refs):
    totals, (tests_ref, gram_ref, sketched_ref) = refs[:members], refs[members:]
    count = sketched_ref.shape[1]
    sums = [
        tree([totals[j][:, (at ^ j) * count : ((at ^ j) + 1) * count] for j in range(members)])
        for at in range(members)
    ]
    sketched_ref[...] = sums[0]
    whole = jnp.concatenate(sums, axis=1)
    parts = []
    rest = whole
    for _ in range(3):
        parts.append(rest.astype(jnp.bfloat16))
        rest = rest - parts[-1].astype(jnp.float32)
    size = whole.shape[0]
    core, gram = None, None
    for at in (2, 1, 0):
        stack = jnp.concatenate([tests_ref[...]] + parts[: 3 - at], axis=0)
        out = lax.dot_general(stack, parts[at], NT, preferred_element_type=jnp.float32)
        pieces = [out[size * p : size * (p + 1), :] for p in range(4 - at)]
        core = pieces[0] if core is None else core + pieces[0]
        inner = pieces[-1]
        for piece in pieces[-2:0:-1]:
            inner = inner + piece
        gram = inner if gram is None else gram + inner
    gram_ref[...] = jnp.concatenate([core, gram], axis=1)


def solve_kernel(scale, near_ref, far_ref, sketched_ref, basis_ref, first_ref):
    gram = near_ref[...] + far_ref[...]
    size, rows = gram.shape[0], 8
    wide = sketched_ref.shape[1]
    core, inner = gram[:, :size], gram[:, size:]
    both = jnp.concatenate([(core + core.T) * 0.5, (inner + inner.T) * 0.5], axis=1)
    left = [both[at : at + rows, :] for at in range(0, size, rows)]
    outs = [[sketched_ref[at : at + rows, :] for at in range(0, size, rows)] for _ in range(2)]
    half = lax.broadcasted_iota(jnp.int32, (rows, 2 * size), 1) < size

    def pick(pair):
        return jnp.where(half, pair[0], pair[1])

    def lane(value, at):
        return jnp.broadcast_to(value[:, at : at + 1], (rows, wide))

    def line(value, at):
        return jnp.broadcast_to(value[at : at + 1, :], (rows, value.shape[1]))

    def forward(lines, lower):
        for j in range(rows):
            for m in range(j + 1, rows):
                lines[m] = lines[m] - lower[m][j] * lines[j]
        return lines

    def backward(lines, lower, inverse):
        lines = [v * r for v, r in zip(lines, inverse)]
        for j in range(rows - 1, 0, -1):
            for m in range(j):
                lines[m] = lines[m] - lower[j][m] * lines[j]
        return lines

    for block in range(size // rows):
        first_row = block * rows
        lowers, inverses, diags = [], [], []
        for s in range(2):
            columns = [lane(left[block], s * size + first_row + j) for j in range(rows)]
            part = [[line(columns[j], m) for j in range(m + 1)] for m in range(rows)]
            lower = [[None] * rows for _ in range(rows)]
            inverse = []
            for j in range(rows):
                inverse.append(1.0 / part[j][j])
                for m in range(j + 1, rows):
                    lower[m][j] = part[m][j] * inverse[j]
                for m in range(j + 1, rows):
                    for q in range(j + 1, m + 1):
                        part[m][q] = part[m][q] - lower[m][j] * part[q][j]
            lowers.append(lower)
            inverses.append(inverse)
            diags.append([part[j][j] for j in range(rows)])
        mixed = [[pick((lowers[0][m][j], lowers[1][m][j])) for j in range(m)] for m in range(rows)]
        lines = forward([line(left[block], j) for j in range(rows)], mixed)
        lines = backward(lines, mixed, [pick(pair) for pair in zip(*inverses)])
        solved = [
            forward([line(outs[s][block], j) for j in range(rows)], lowers[s]) for s in range(2)
        ]
        steps = [backward(list(solved[s]), lowers[s], inverses[s]) for s in range(2)]
        for below in range(block + 1, size // rows):
            for j in range(rows):
                pair = [lane(left[below], s * size + first_row + j) for s in range(2)]
                for s in range(2):
                    outs[s][below] = outs[s][below] - pair[s] * steps[s][j]
                if j == 0:
                    update = pick(pair) * lines[j]
                else:
                    update = update + pick(pair) * lines[j]
            left[below] = left[below] - update
        for s, out_ref in enumerate((first_ref, basis_ref)):
            for j in range(rows):
                value = solved[s][j] * (lax.rsqrt(diags[s][j]) * scale)
                out_ref[first_row + j : first_row + j + 1, :] = value[:1, :]


def per_device(embeddings, sketch, rows, cols):
    count, width = embeddings.shape
    columns = sketch.shape[1]
    gamma = 3.0 / width
    near = 2 if cols % 2 == 0 else 1
    members, others = rows // 2 * near, 2 * (cols // near)
    devices = rows * cols

    def swap(value, mask):
        return lax.ppermute(value, AXES, [(i, i ^ mask) for i in range(devices)])

    tests = sketch.T
    packed_rows = count + columns * count // width
    packed = pl.pallas_call(
        pack_kernel,
        out_shape=jax.ShapeDtypeStruct((packed_rows, width), embeddings.dtype),
        in_specs=[VMEM, VMEM],
        out_specs=VMEM,
        compiler_params=pltpu.CompilerParams(vmem_limit_bytes=4 << 20),
        name="pack",
    )(embeddings, tests)
    own_masks = [2 * cols * x + l for x in range(rows // 2) for l in range(near)][1:]
    far_masks = [near * j for j in range(1, cols // near)]
    own = [packed] + [swap(packed, m) for m in own_masks]
    far = [packed] + [swap(packed, m) for m in far_masks]
    facing = far + [swap(block, cols) for block in far]
    wide = members * count
    total, own_tests = pl.pallas_call(
        functools.partial(tile_kernel, members, others, 256, gamma),
        out_shape=(
            jax.ShapeDtypeStruct((columns, wide), jnp.float32),
            jax.ShapeDtypeStruct((columns, wide), sketch.dtype),
        ),
        in_specs=[VMEM] * (members + others - 1),
        out_specs=(VMEM, VMEM),
        scratch_shapes=[
            pltpu.VMEM((wide, width), embeddings.dtype),
            pltpu.VMEM((8, wide), jnp.float32),
            pltpu.VMEM((others * count, width), embeddings.dtype),
            pltpu.VMEM((columns, others * count), sketch.dtype),
        ],
        compiler_params=pltpu.CompilerParams(vmem_limit_bytes=24 << 20),
        name="tile",
    )(*own, *facing[1:])
    totals = [total] + [swap(total, m) for m in own_masks]
    gram, sketched = pl.pallas_call(
        functools.partial(gram_kernel, members),
        out_shape=(
            jax.ShapeDtypeStruct((columns, 2 * columns), jnp.float32),
            jax.ShapeDtypeStruct((columns, count), jnp.float32),
        ),
        in_specs=[VMEM] * (members + 1),
        out_specs=(VMEM, VMEM),
        compiler_params=pltpu.CompilerParams(vmem_limit_bytes=24 << 20),
        name="gram",
    )(*totals, own_tests)
    masks = [cols]
    mask = near
    while mask < cols:
        masks.append(mask)
        mask *= 2
    for mask in masks[:-1]:
        gram = gram + swap(gram, mask)
    scale = float(devices * count) ** 0.5
    basis, first = pl.pallas_call(
        functools.partial(solve_kernel, scale),
        out_shape=(jax.ShapeDtypeStruct((columns, count), jnp.float32),) * 2,
        in_specs=[VMEM] * 3,
        out_specs=(VMEM, VMEM),
        compiler_params=pltpu.CompilerParams(vmem_limit_bytes=8 << 20),
        name="solve",
    )(gram, swap(gram, masks[-1]), sketched)
    return basis.T, first.T


def solution(mesh):
    placed = P(AXES, None)
    return jax.shard_map(
        functools.partial(per_device, rows=mesh.shape["row"], cols=mesh.shape["col"]),
        mesh=mesh,
        in_specs=(placed, placed),
        out_specs=(placed, placed),
        check_vma=False,
    )
```

```python
import functools

import jax
import jax.numpy as jnp
from jax import lax
from jax.experimental import pallas as pl
from jax.experimental.pallas import tpu as pltpu
from jax.sharding import PartitionSpec as P

AXES = ("row", "col")
NT = (((1,), (1,)), ((), ()))
NN = (((1,), (0,)), ((), ()))
LOG2E = 1.4426950408889634
VMEM = pl.BlockSpec(memory_space=pltpu.VMEM)
HBM = pl.BlockSpec(memory_space=pltpu.HBM)


def params(mebibytes):
    return pltpu.CompilerParams(vmem_limit_bytes=mebibytes << 20)


def tree(values):
    while len(values) > 1:
        values = [a + b for a, b in zip(values[::2], values[1::2])]
    return values[0]


def pack_kernel(points_ref, tests_ref, out_ref, sems):
    count, width = points_ref.shape
    pieces = width // count
    depth = tests_ref.shape[0] // pieces
    copies = [pltpu.make_async_copy(points_ref, out_ref.at[:count, :], sems.at[0])]
    for piece in range(pieces):
        copies.append(
            pltpu.make_async_copy(
                tests_ref.at[piece * depth : (piece + 1) * depth, :],
                out_ref.at[count:, piece * count : (piece + 1) * count],
                sems.at[piece + 1],
            )
        )
    for copy in copies:
        copy.start()
    for copy in copies:
        copy.wait()


def put_tests(pack, tests, at):
    height, width = pack.shape
    columns = tests.shape[0]
    count = height * width // (width + columns)
    pieces = width // count
    depth = columns // pieces
    for piece in range(pieces):
        tests[piece * depth : (piece + 1) * depth, at * count : (at + 1) * count] = pack[
            count:, piece * count : (piece + 1) * count
        ]


def weights_of(points, rate):
    wide = points.astype(jnp.float32)
    return jnp.sum(wide * wide, axis=1, keepdims=True) * rate


def accumulate(packs, total, own_ref, weights_ref, points, tests, chunk, rate):
    count = points.shape[0] // len(packs)
    for at, pack in enumerate(packs):
        points[at * count : (at + 1) * count, :] = pack[:count, :]
        put_tests(pack, tests, at)
    for start in range(0, len(packs) * count, chunk):
        block = points[start : start + chunk, :]
        cross = lax.dot_general(block, own_ref[...], NT, preferred_element_type=jnp.float32)
        power = cross * (2.0 * rate) - (weights_of(block, rate) + weights_ref[:1, :])
        tile = jnp.exp2(power).astype(jnp.bfloat16)
        part = lax.dot_general(
            tests[:, start : start + chunk], tile, NN, preferred_element_type=jnp.float32
        )
        total = part if total is None else total + part
    return total


def near_kernel(members, chunk, rate, *refs):
    total_ref, tests_ref, own_ref, weights_ref, points, tests = refs[-6:]
    packs = refs[:-6]
    count = own_ref.shape[0] // members
    for at in range(members):
        own_ref[at * count : (at + 1) * count, :] = packs[at][:count, :]
        put_tests(packs[at], tests_ref, at)
        column = weights_of(packs[at][:count, :], rate)
        weights_ref[:, at * count : (at + 1) * count] = jnp.broadcast_to(column, (count, count)).T[:8]
    facing = packs[:1] + packs[members:]
    total_ref[...] = accumulate(facing, None, own_ref, weights_ref, points, tests, chunk, rate)


def far_kernel(chunk, rate, near_ref, own_ref, weights_ref, *refs):
    packs, (total_ref, points, tests) = refs[:-3], refs[-3:]
    total_ref[...] = accumulate(
        packs, near_ref[...], own_ref, weights_ref, points, tests, chunk, rate
    )


def gram_kernel(members, near, *refs):
    totals, (tests_ref, gram_ref, sketched_ref, whole, tests) = refs[:members], refs[members:]
    count = sketched_ref.shape[1]
    here = lax.axis_index("row") // 2 * near + lax.axis_index("col") % near
    for at in range(members):
        part = tree([
            totals[j][:, (at ^ j) * count : ((at ^ j) + 1) * count] for j in range(members)
        ])
        if at == 0:
            sketched_ref[...] = part
        place = pl.ds(pl.multiple_of((here ^ at) * count, count), count)
        whole[:, place] = part
        tests[:, place] = tests_ref[:, at * count : (at + 1) * count]
    parts = []
    rest = whole[...]
    size = rest.shape[0]
    for _ in range(3):
        parts.append(rest.astype(jnp.bfloat16))
        rest = rest - parts[-1].astype(jnp.float32)
    core, gram = None, None
    for at in (2, 1, 0):
        stack = jnp.concatenate([tests[...]] + parts[: 3 - at], axis=0)
        out = lax.dot_general(stack, parts[at], NT, preferred_element_type=jnp.float32)
        pieces = [out[size * p : size * (p + 1), :] for p in range(4 - at)]
        core = pieces[0] if core is None else core + pieces[0]
        inner = pieces[-1]
        for piece in pieces[-2:0:-1]:
            inner = inner + piece
        gram = inner if gram is None else gram + inner
    gram_ref[...] = jnp.concatenate([core, gram], axis=1)


def solve_kernel(scale, *refs):
    grams, (sketched_ref, basis_ref, first_ref) = refs[:-3], refs[-3:]
    gram = tree([ref[...] for ref in grams])
    size, rows = gram.shape[0], 8
    count = size // rows
    core, inner = gram[:, :size], gram[:, size:]
    both = jnp.concatenate([(core + core.T) * 0.5, (inner + inner.T) * 0.5], axis=1)
    sketched = sketched_ref[...]
    sides = [jnp.concatenate([sketched[:, at : at + size]] * 2, axis=1) for at in (0, size)]
    stacks = [[m[at : at + rows, :] for at in range(0, size, rows)] for m in [both] + sides]
    half = lax.broadcasted_iota(jnp.int32, (rows, 2 * size), 1) < size

    def spread(value):
        return jnp.broadcast_to(value, (rows, 2 * size))

    def column(value, at):
        left, right = value[:, at : at + 1], value[:, size + at : size + at + 1]
        return jnp.where(half, spread(left), spread(right))

    outs = [[], []]
    for block in range(count):
        first_row = block * rows
        columns = [column(stacks[0][block], first_row + j) for j in range(rows)]
        part = [[spread(columns[j][m : m + 1, :]) for j in range(m + 1)] for m in range(rows)]
        lower = [[None] * rows for _ in range(rows)]
        inverse = []
        for j in range(rows):
            inverse.append(1.0 / part[j][j])
            for m in range(j + 1, rows):
                lower[m][j] = part[m][j] * inverse[j]
            for m in range(j + 1, rows):
                for q in range(j + 1, m + 1):
                    part[m][q] = part[m][q] - lower[m][j] * part[q][j]
        steps = []
        for stack in stacks:
            lines = [spread(stack[block][j : j + 1, :]) for j in range(rows)]
            for j in range(rows):
                for m in range(j + 1, rows):
                    lines[m] = lines[m] - lower[m][j] * lines[j]
            if steps:
                for j in range(rows):
                    root = lax.rsqrt(part[j][j]) * scale
                    outs[len(steps) - 1].append((lines[j] * root)[:1, :])
            lines = [line * r for line, r in zip(lines, inverse)]
            for j in range(rows - 1, 0, -1):
                for m in range(j):
                    lines[m] = lines[m] - lower[j][m] * lines[j]
            steps.append(lines)
        for below in range(block + 1, count):
            factors = [column(stacks[0][below], first_row + j) for j in range(rows)]
            for stack, lines in zip(stacks, steps):
                update = factors[0] * lines[0]
                for j in range(1, rows):
                    update = update + factors[j] * lines[j]
                stack[below] = stack[below] - update
    left, right = [jnp.concatenate(lines, axis=0) for lines in outs]
    first_ref[...] = jnp.concatenate([left[:, :size], right[:, :size]], axis=1)
    basis_ref[...] = jnp.concatenate([left[:, size:], right[:, size:]], axis=1)


def per_device(embeddings, sketch, rows, cols):
    count, width = embeddings.shape
    columns = sketch.shape[1]
    rate = 3.0 / width * LOG2E
    near = 2 if cols % 2 == 0 else 1
    members, others = rows // 2 * near, cols // near
    devices = rows * cols
    like = jax.ShapeDtypeStruct
    wide, deep = members * count, others * count
    chunk = min(deep, 512)

    def swap(value, mask):
        return lax.ppermute(value, AXES, [(i, i ^ mask) for i in range(devices)])

    packed = pl.pallas_call(
        pack_kernel,
        out_shape=like((count + columns * count // width, width), embeddings.dtype),
        in_specs=[HBM, HBM],
        out_specs=VMEM,
        scratch_shapes=[pltpu.SemaphoreType.DMA((1 + width // count,))],
        compiler_params=params(4),
        name="pack",
    )(embeddings, sketch.T)
    own_masks = [2 * cols * x + l for x in range(rows // 2) for l in range(near)][1:]
    far_masks = [near * j for j in range(1, others)]
    own = [packed] + [swap(packed, m) for m in own_masks]
    facing = [packed] + [swap(packed, m) for m in far_masks]
    across = [swap(block, cols) for block in facing]
    facing_scratch = [
        pltpu.VMEM((deep, width), embeddings.dtype),
        pltpu.VMEM((columns, deep), sketch.dtype),
    ]
    cost = pl.CostEstimate(
        flops=2 * wide * deep * (width + columns),
        bytes_accessed=2 * (wide + deep) * width,
        transcendentals=wide * deep,
    )
    near_total, own_tests, own_points, weights = pl.pallas_call(
        functools.partial(near_kernel, members, chunk, rate),
        out_shape=(
            like((columns, wide), jnp.float32),
            like((columns, wide), sketch.dtype),
            like((wide, width), embeddings.dtype),
            like((8, wide), jnp.float32),
        ),
        in_specs=[VMEM] * (members + others - 1),
        out_specs=(VMEM,) * 4,
        scratch_shapes=facing_scratch,
        compiler_params=params(24),
        cost_estimate=cost,
        name="near",
    )(*own, *facing[1:])
    total = pl.pallas_call(
        functools.partial(far_kernel, chunk, rate),
        out_shape=like((columns, wide), jnp.float32),
        in_specs=[VMEM] * (3 + others),
        out_specs=VMEM,
        scratch_shapes=facing_scratch,
        compiler_params=params(24),
        cost_estimate=cost,
        name="far",
    )(near_total, own_points, weights, *across)
    totals = [total] + [swap(total, m) for m in own_masks]
    gram, sketched = pl.pallas_call(
        functools.partial(gram_kernel, members, near),
        out_shape=(
            like((columns, 2 * columns), jnp.float32),
            like((columns, count), jnp.float32),
        ),
        in_specs=[VMEM] * (members + 1),
        out_specs=(VMEM, VMEM),
        scratch_shapes=[
            pltpu.VMEM((columns, wide), jnp.float32),
            pltpu.VMEM((columns, wide), sketch.dtype),
        ],
        compiler_params=params(24),
        name="gram",
    )(*totals, own_tests)
    gram = gram + swap(gram, cols)
    mask = near
    grams = [gram]
    while mask < cols:
        grams = [tree(grams)]
        masks = [mask, 2 * mask, 3 * mask] if 2 * mask < cols else [mask]
        grams += [swap(grams[0], m) for m in masks]
        mask *= len(masks) + 1
    scale = float(devices * count) ** 0.5
    basis, first = pl.pallas_call(
        functools.partial(solve_kernel, scale),
        out_shape=(like((columns, count), jnp.float32),) * 2,
        in_specs=[VMEM] * (len(grams) + 1),
        out_specs=(VMEM, VMEM),
        compiler_params=params(8),
        name="solve",
    )(*grams, sketched)
    return basis.T, first.T


def solution(mesh):
    placed = P(AXES, None)
    return jax.shard_map(
        functools.partial(per_device, rows=mesh.shape["row"], cols=mesh.shape["col"]),
        mesh=mesh,
        in_specs=(placed, placed),
        out_specs=(placed, placed),
        check_vma=False,
    )
```

```python
import functools

import jax
import jax.numpy as jnp
from jax import lax
from jax.experimental import pallas as pl
from jax.experimental.pallas import tpu as pltpu
from jax.sharding import PartitionSpec as P

AXES = ("row", "col")
NT = (((1,), (1,)), ((), ()))
NN = (((1,), (0,)), ((), ()))
LOG2E = 1.4426950408889634
VMEM = pl.BlockSpec(memory_space=pltpu.VMEM)
HBM = pl.BlockSpec(memory_space=pltpu.HBM)


def params(mebibytes):
    return pltpu.CompilerParams(vmem_limit_bytes=mebibytes << 20)


def tree(values):
    while len(values) > 1:
        values = [a + b for a, b in zip(values[::2], values[1::2])]
    return values[0]


def pack_kernel(points_ref, tests_ref, out_ref, sems):
    count, width = points_ref.shape
    pieces = width // count
    depth = tests_ref.shape[0] // pieces
    copies = [pltpu.make_async_copy(points_ref, out_ref.at[:count, :], sems.at[0])]
    for piece in range(pieces):
        copies.append(
            pltpu.make_async_copy(
                tests_ref.at[piece * depth : (piece + 1) * depth, :],
                out_ref.at[count:, piece * count : (piece + 1) * count],
                sems.at[piece + 1],
            )
        )
    for copy in copies:
        copy.start()
    for copy in copies:
        copy.wait()


def put_tests(pack, tests, at):
    height, width = pack.shape
    columns = tests.shape[0]
    count = height * width // (width + columns)
    pieces = width // count
    depth = columns // pieces
    for piece in range(pieces):
        tests[piece * depth : (piece + 1) * depth, at * count : (at + 1) * count] = pack[
            count:, piece * count : (piece + 1) * count
        ]


def weights_of(points, rate):
    wide = points.astype(jnp.float32)
    return jnp.sum(wide * wide, axis=1, keepdims=True) * rate


def accumulate(packs, total, own_ref, weights_ref, points, tests, chunk, rate):
    count = points.shape[0] // len(packs)
    for at, pack in enumerate(packs):
        points[at * count : (at + 1) * count, :] = pack[:count, :]
        put_tests(pack, tests, at)
    for start in range(0, len(packs) * count, chunk):
        block = points[start : start + chunk, :]
        cross = lax.dot_general(block, own_ref[...], NT, preferred_element_type=jnp.float32)
        power = cross * (2.0 * rate) - (weights_of(block, rate) + weights_ref[:1, :])
        tile = jnp.exp2(power).astype(jnp.bfloat16)
        part = lax.dot_general(
            tests[:, start : start + chunk], tile, NN, preferred_element_type=jnp.float32
        )
        total = part if total is None else total + part
    return total


def near_kernel(members, chunk, rate, *refs):
    total_ref, tests_ref, own_ref, weights_ref, points, tests = refs[-6:]
    packs = refs[:-6]
    count = own_ref.shape[0] // members
    for at in range(members):
        own_ref[at * count : (at + 1) * count, :] = packs[at][:count, :]
        put_tests(packs[at], tests_ref, at)
        column = weights_of(packs[at][:count, :], rate)
        weights_ref[:, at * count : (at + 1) * count] = jnp.broadcast_to(column, (count, count)).T[:8]
    facing = packs[:1] + packs[:members-1:-1]
    total_ref[...] = accumulate(facing, None, own_ref, weights_ref, points, tests, chunk, rate)


def far_kernel(chunk, rate, near_ref, own_ref, weights_ref, *refs):
    packs, (total_ref, points, tests) = refs[:-3], refs[-3:]
    total_ref[...] = accumulate(
        packs, near_ref[...], own_ref, weights_ref, points, tests, chunk, rate
    )


def gram_kernel(members, near, *refs):
    totals, (tests_ref, gram_ref, sketched_ref, whole, tests) = refs[members - 1 :: -1], refs[members:]
    count = sketched_ref.shape[1]
    here = lax.axis_index("row") // 2 * near + lax.axis_index("col") % near
    for at in range(members):
        part = tree([
            totals[j][:, (at ^ j) * count : ((at ^ j) + 1) * count] for j in range(members)
        ])
        if at == 0:
            sketched_ref[...] = part
        place = pl.ds(pl.multiple_of((here ^ at) * count, count), count)
        whole[:, place] = part
        tests[:, place] = tests_ref[:, at * count : (at + 1) * count]
    parts = []
    rest = whole[...]
    size = rest.shape[0]
    for _ in range(3):
        parts.append(rest.astype(jnp.bfloat16))
        rest = rest - parts[-1].astype(jnp.float32)
    core, gram = None, None
    for at in (2, 1, 0):
        stack = jnp.concatenate([tests[...]] + parts[: 3 - at], axis=0)
        out = lax.dot_general(stack, parts[at], NT, preferred_element_type=jnp.float32)
        pieces = [out[size * p : size * (p + 1), :] for p in range(4 - at)]
        core = pieces[0] if core is None else core + pieces[0]
        inner = pieces[-1]
        for piece in pieces[-2:0:-1]:
            inner = inner + piece
        gram = inner if gram is None else gram + inner
    gram_ref[...] = jnp.concatenate([core, gram], axis=1)


def solve_kernel(scale, *refs):
    grams, (sketched_ref, basis_ref, first_ref) = refs[:-3], refs[-3:]
    gram = tree([ref[...] for ref in grams[::-1]])
    size, rows = gram.shape[0], 8
    count = size // rows
    core, inner = gram[:, :size], gram[:, size:]
    both = jnp.concatenate([(core + core.T) * 0.5, (inner + inner.T) * 0.5], axis=1)
    sketched = sketched_ref[...]
    sides = [jnp.concatenate([sketched[:, at : at + size]] * 2, axis=1) for at in (0, size)]
    stacks = [[m[at : at + rows, :] for at in range(0, size, rows)] for m in [both] + sides]
    half = lax.broadcasted_iota(jnp.int32, (rows, 2 * size), 1) < size

    def spread(value):
        return jnp.broadcast_to(value, (rows, 2 * size))

    def column(value, at):
        left, right = value[:, at : at + 1], value[:, size + at : size + at + 1]
        return jnp.where(half, spread(left), spread(right))

    outs = [[], []]
    for block in range(count):
        first_row = block * rows
        columns = [column(stacks[0][block], first_row + j) for j in range(rows)]
        part = [[spread(columns[j][m : m + 1, :]) for j in range(m + 1)] for m in range(rows)]
        lower = [[None] * rows for _ in range(rows)]
        inverse = []
        for j in range(rows):
            inverse.append(1.0 / part[j][j])
            for m in range(j + 1, rows):
                lower[m][j] = part[m][j] * inverse[j]
            for m in range(j + 1, rows):
                for q in range(j + 1, m + 1):
                    part[m][q] = part[m][q] - lower[m][j] * part[q][j]
        steps = []
        for stack in stacks:
            lines = [spread(stack[block][j : j + 1, :]) for j in range(rows)]
            for j in range(rows):
                for m in range(j + 1, rows):
                    lines[m] = lines[m] - lower[m][j] * lines[j]
            if steps:
                for j in range(rows):
                    root = lax.rsqrt(part[j][j]) * scale
                    outs[len(steps) - 1].append((lines[j] * root)[:1, :])
            lines = [line * r for line, r in zip(lines, inverse)]
            for j in range(rows - 1, 0, -1):
                for m in range(j):
                    lines[m] = lines[m] - lower[j][m] * lines[j]
            steps.append(lines)
        for below in range(block + 1, count):
            factors = [column(stacks[0][below], first_row + j) for j in range(rows)]
            for stack, lines in zip(stacks, steps):
                update = factors[0] * lines[0]
                for j in range(1, rows):
                    update = update + factors[j] * lines[j]
                stack[below] = stack[below] - update
    left, right = [jnp.concatenate(lines, axis=0) for lines in outs]
    first_ref[...] = jnp.concatenate([left[:, :size], right[:, :size]], axis=1)
    basis_ref[...] = jnp.concatenate([left[:, size:], right[:, size:]], axis=1)


def per_device(embeddings, sketch, rows, cols):
    count, width = embeddings.shape
    columns = sketch.shape[1]
    rate = 3.0 / width * LOG2E
    near = 2 if cols % 2 == 0 else 1
    members, others = rows // 2 * near, cols // near
    devices = rows * cols
    like = jax.ShapeDtypeStruct
    wide, deep = members * count, others * count
    chunk = min(deep, 512)

    def swap(value, mask):
        return lax.ppermute(value, AXES, [(i, i ^ mask) for i in range(devices)])

    def swaps(value, masks):
        return [swap(value, mask) for mask in masks]

    packed = pl.pallas_call(
        pack_kernel,
        out_shape=like((count + columns * count // width, width), embeddings.dtype),
        in_specs=[HBM, HBM],
        out_specs=VMEM,
        scratch_shapes=[pltpu.SemaphoreType.DMA((1 + width // count,))],
        compiler_params=params(4),
        name="pack",
    )(embeddings, sketch.T)
    own_masks = [2 * cols * x + l for x in range(rows // 2) for l in range(near)][1:]
    far_masks = [near * j for j in range(1, others)]
    facing = [packed] + swaps(packed, far_masks)
    own = [packed] + swaps(packed, own_masks)
    across = [swap(block, cols) for block in facing]
    facing_scratch = [
        pltpu.VMEM((deep, width), embeddings.dtype),
        pltpu.VMEM((columns, deep), sketch.dtype),
    ]
    cost = pl.CostEstimate(
        flops=2 * wide * deep * (width + columns),
        bytes_accessed=2 * (wide + deep) * width,
        transcendentals=wide * deep,
    )
    near_total, own_tests, own_points, weights = pl.pallas_call(
        functools.partial(near_kernel, members, chunk, rate),
        out_shape=(
            like((columns, wide), jnp.float32),
            like((columns, wide), sketch.dtype),
            like((wide, width), embeddings.dtype),
            like((8, wide), jnp.float32),
        ),
        in_specs=[VMEM] * (members + others - 1),
        out_specs=(VMEM,) * 4,
        scratch_shapes=facing_scratch,
        compiler_params=params(24),
        cost_estimate=cost,
        name="near",
    )(*own, *facing[:0:-1])
    total = pl.pallas_call(
        functools.partial(far_kernel, chunk, rate),
        out_shape=like((columns, wide), jnp.float32),
        in_specs=[VMEM] * (3 + others),
        out_specs=VMEM,
        scratch_shapes=facing_scratch,
        compiler_params=params(24),
        cost_estimate=cost,
        name="far",
    )(near_total, own_points, weights, *across[::-1])
    totals = [total] + swaps(total, own_masks)
    gram, sketched = pl.pallas_call(
        functools.partial(gram_kernel, members, near),
        out_shape=(
            like((columns, 2 * columns), jnp.float32),
            like((columns, count), jnp.float32),
        ),
        in_specs=[VMEM] * (members + 1),
        out_specs=(VMEM, VMEM),
        scratch_shapes=[
            pltpu.VMEM((columns, wide), jnp.float32),
            pltpu.VMEM((columns, wide), sketch.dtype),
        ],
        compiler_params=params(24),
        name="gram",
    )(*totals[::-1], own_tests)
    gram = gram + swap(gram, cols)
    mask = near
    grams = [gram]
    while mask < cols:
        grams = [tree(grams)]
        masks = [mask, 2 * mask, 3 * mask] if 2 * mask < cols else [mask]
        grams += swaps(grams[0], masks)
        mask *= len(masks) + 1
    scale = float(devices * count) ** 0.5
    basis, first = pl.pallas_call(
        functools.partial(solve_kernel, scale),
        out_shape=(like((columns, count), jnp.float32),) * 2,
        in_specs=[VMEM] * (len(grams) + 1),
        out_specs=(VMEM, VMEM),
        compiler_params=params(8),
        name="solve",
    )(*grams[::-1], sketched)
    return basis.T, first.T


def solution(mesh):
    placed = P(AXES, None)
    return jax.shard_map(
        functools.partial(per_device, rows=mesh.shape["row"], cols=mesh.shape["col"]),
        mesh=mesh,
        in_specs=(placed, placed),
        out_specs=(placed, placed),
        check_vma=False,
    )
```

```python
import functools

import jax
import jax.numpy as jnp
from jax import lax
from jax.experimental import pallas as pl
from jax.experimental.pallas import tpu as pltpu
from jax.sharding import PartitionSpec as P

AXES = ("row", "col")
NT = (((1,), (1,)), ((), ()))
NN = (((1,), (0,)), ((), ()))
LOG2E = 1.4426950408889634
MARGIN = 2.0**-7
VMEM = pl.BlockSpec(memory_space=pltpu.VMEM)
HBM = pl.BlockSpec(memory_space=pltpu.HBM)


def params(mebibytes):
    return pltpu.CompilerParams(vmem_limit_bytes=mebibytes << 20)


def tree(values):
    while len(values) > 1:
        values = [a + b for a, b in zip(values[::2], values[1::2])]
    return values[0]


def pack_kernel(points_ref, tests_ref, out_ref, sems):
    count, width = points_ref.shape
    pieces = width // count
    depth = tests_ref.shape[0] // pieces
    copies = [pltpu.make_async_copy(points_ref, out_ref.at[:count, :], sems.at[0])]
    for piece in range(pieces):
        copies.append(
            pltpu.make_async_copy(
                tests_ref.at[piece * depth : (piece + 1) * depth, :],
                out_ref.at[count:, piece * count : (piece + 1) * count],
                sems.at[piece + 1],
            )
        )
    for copy in copies:
        copy.start()
    for copy in copies:
        copy.wait()


def put_tests(pack, tests, at):
    height, width = pack.shape
    columns = tests.shape[0]
    count = height * width // (width + columns)
    pieces = width // count
    depth = columns // pieces
    for piece in range(pieces):
        tests[piece * depth : (piece + 1) * depth, at * count : (at + 1) * count] = pack[
            count:, piece * count : (piece + 1) * count
        ]


def weights_of(points, rate):
    wide = points.astype(jnp.float32)
    return jnp.sum(wide * wide, axis=1, keepdims=True) * rate


def accumulate(packs, total, own_ref, weights_ref, points, tests, chunk, rate):
    count = points.shape[0] // len(packs)
    for at, pack in enumerate(packs):
        points[at * count : (at + 1) * count, :] = pack[:count, :]
        put_tests(pack, tests, at)
    for start in range(0, len(packs) * count, chunk):
        block = points[start : start + chunk, :]
        cross = lax.dot_general(block, own_ref[...], NT, preferred_element_type=jnp.float32)
        power = cross * (2.0 * rate) - (weights_of(block, rate) + weights_ref[:1, :])
        tile = jnp.exp2(power).astype(jnp.bfloat16)
        part = lax.dot_general(
            tests[:, start : start + chunk], tile, NN, preferred_element_type=jnp.float32
        )
        total = part if total is None else total + part
    return total


def near_kernel(members, chunk, rate, *refs):
    total_ref, tests_ref, own_ref, weights_ref, points, tests = refs[-6:]
    packs = refs[:-6]
    count = own_ref.shape[0] // members
    for at in range(members):
        own_ref[at * count : (at + 1) * count, :] = packs[at][:count, :]
        put_tests(packs[at], tests_ref, at)
        column = weights_of(packs[at][:count, :], rate)
        weights_ref[:, at * count : (at + 1) * count] = jnp.broadcast_to(column, (count, count)).T[:8]
    facing = packs[:1] + packs[:members-1:-1]
    total_ref[...] = accumulate(facing, None, own_ref, weights_ref, points, tests, chunk, rate)


def far_kernel(chunk, rate, near_ref, own_ref, weights_ref, *refs):
    packs, (total_ref, points, tests) = refs[:-3], refs[-3:]
    total_ref[...] = accumulate(
        packs, near_ref[...], own_ref, weights_ref, points, tests, chunk, rate
    )


def products(tests, whole):
    parts = []
    rest = whole
    size = whole.shape[0]
    for _ in range(3):
        parts.append(rest.astype(jnp.bfloat16))
        rest = rest - parts[-1].astype(jnp.float32)
    core, gram = None, None
    for at in (2, 1, 0):
        stack = jnp.concatenate([tests] + parts[: 3 - at], axis=0)
        out = lax.dot_general(stack, parts[at], NT, preferred_element_type=jnp.float32)
        pieces = [out[size * p : size * (p + 1), :] for p in range(4 - at)]
        core = pieces[0] if core is None else core + pieces[0]
        inner = pieces[-1]
        for piece in pieces[-2:0:-1]:
            inner = inner + piece
        gram = inner if gram is None else gram + inner
    return core, gram


def again_kernel(first_ref, gram_ref):
    first = first_ref[...]
    _, gram = products(first.astype(jnp.bfloat16), first)
    gram_ref[...] = jnp.concatenate([gram, gram], axis=1)


def gram_kernel(members, near, *refs):
    totals, (tests_ref, gram_ref, sketched_ref, whole, tests) = refs[members - 1 :: -1], refs[members:]
    count = sketched_ref.shape[1]
    here = lax.axis_index("row") // 2 * near + lax.axis_index("col") % near
    for at in range(members):
        part = tree([
            totals[j][:, (at ^ j) * count : ((at ^ j) + 1) * count] for j in range(members)
        ])
        if at == 0:
            sketched_ref[...] = part
        place = pl.ds(pl.multiple_of((here ^ at) * count, count), count)
        whole[:, place] = part
        tests[:, place] = tests_ref[:, at * count : (at + 1) * count]
    core, gram = products(tests[...], whole[...])
    gram_ref[...] = jnp.concatenate([core, gram], axis=1)


def solve_kernel(scale, *refs):
    grams, (sketched_ref, basis_ref, first_ref, margin_ref) = refs[:-4], refs[-4:]
    gram = tree([ref[...] for ref in grams[::-1]])
    size, rows = gram.shape[0], 8
    count = size // rows
    core, inner = gram[:, :size], gram[:, size:]
    both = jnp.concatenate([(core + core.T) * 0.5, (inner + inner.T) * 0.5], axis=1)
    sketched = sketched_ref[...]
    sides = [jnp.concatenate([sketched[:, at : at + size]] * 2, axis=1) for at in (0, size)]
    stacks = [[m[at : at + rows, :] for at in range(0, size, rows)] for m in [both] + sides]
    half = lax.broadcasted_iota(jnp.int32, (rows, 2 * size), 1) < size

    def spread(value):
        return jnp.broadcast_to(value, (rows, 2 * size))

    def column(value, at):
        left, right = value[:, at : at + 1], value[:, size + at : size + at + 1]
        return jnp.where(half, spread(left), spread(right))

    place = lax.broadcasted_iota(jnp.int32, (rows, 2 * size), 1)
    pivots = jnp.ones((rows, 2 * size), jnp.float32)
    outs = [[], []]
    for block in range(count):
        first_row = block * rows
        columns = [column(stacks[0][block], first_row + j) for j in range(rows)]
        part = [[spread(columns[j][m : m + 1, :]) for j in range(m + 1)] for m in range(rows)]
        lower = [[None] * rows for _ in range(rows)]
        inverse = []
        for j in range(rows):
            inverse.append(1.0 / part[j][j])
            for m in range(j + 1, rows):
                lower[m][j] = part[m][j] * inverse[j]
            for m in range(j + 1, rows):
                for q in range(j + 1, m + 1):
                    part[m][q] = part[m][q] - lower[m][j] * part[q][j]
        for j in range(rows):
            pivots = jnp.where(place == size + first_row + j, part[j][j], pivots)
        steps = []
        for stack in stacks:
            lines = [spread(stack[block][j : j + 1, :]) for j in range(rows)]
            for j in range(rows):
                for m in range(j + 1, rows):
                    lines[m] = lines[m] - lower[m][j] * lines[j]
            if steps:
                for j in range(rows):
                    root = lax.rsqrt(part[j][j]) * scale
                    outs[len(steps) - 1].append((lines[j] * root)[:1, :])
            lines = [line * r for line, r in zip(lines, inverse)]
            for j in range(rows - 1, 0, -1):
                for m in range(j):
                    lines[m] = lines[m] - lower[j][m] * lines[j]
            steps.append(lines)
        for below in range(block + 1, count):
            factors = [column(stacks[0][below], first_row + j) for j in range(rows)]
            for stack, lines in zip(stacks, steps):
                update = factors[0] * lines[0]
                for j in range(1, rows):
                    update = update + factors[j] * lines[j]
                stack[below] = stack[below] - update
    at_row = lax.broadcasted_iota(jnp.int32, both.shape, 0)
    at_lane = lax.broadcasted_iota(jnp.int32, both.shape, 1)
    diagonal = jnp.sum(jnp.where(at_lane == at_row + size, both, 0.0), axis=0, keepdims=True)
    kept = jnp.where(at_lane[:1] < size, 1.0, pivots[:1] / diagonal)
    margin_ref[0, 0] = jnp.min(kept)
    left, right = [jnp.concatenate(lines, axis=0) for lines in outs]
    first_ref[...] = jnp.concatenate([left[:, :size], right[:, :size]], axis=1)
    basis_ref[...] = jnp.concatenate([left[:, size:], right[:, size:]], axis=1)


def per_device(embeddings, sketch, rows, cols):
    count, width = embeddings.shape
    columns = sketch.shape[1]
    rate = 3.0 / width * LOG2E
    near = 2 if cols % 2 == 0 else 1
    members, others = rows // 2 * near, cols // near
    devices = rows * cols
    like = jax.ShapeDtypeStruct
    wide, deep = members * count, others * count
    chunk = min(deep, 512)

    def swap(value, mask):
        return lax.ppermute(value, AXES, [(i, i ^ mask) for i in range(devices)])

    def swaps(value, masks):
        return [swap(value, mask) for mask in masks]

    packed = pl.pallas_call(
        pack_kernel,
        out_shape=like((count + columns * count // width, width), embeddings.dtype),
        in_specs=[HBM, HBM],
        out_specs=VMEM,
        scratch_shapes=[pltpu.SemaphoreType.DMA((1 + width // count,))],
        compiler_params=params(4),
        name="pack",
    )(embeddings, sketch.T)
    own_masks = [2 * cols * x + l for x in range(rows // 2) for l in range(near)][1:]
    far_masks = [near * j for j in range(1, others)]
    facing = [packed] + swaps(packed, far_masks)
    own = [packed] + swaps(packed, own_masks)
    across = [swap(block, cols) for block in facing]
    facing_scratch = [
        pltpu.VMEM((deep, width), embeddings.dtype),
        pltpu.VMEM((columns, deep), sketch.dtype),
    ]
    cost = pl.CostEstimate(
        flops=2 * wide * deep * (width + columns),
        bytes_accessed=2 * (wide + deep) * width,
        transcendentals=wide * deep,
    )
    near_total, own_tests, own_points, weights = pl.pallas_call(
        functools.partial(near_kernel, members, chunk, rate),
        out_shape=(
            like((columns, wide), jnp.float32),
            like((columns, wide), sketch.dtype),
            like((wide, width), embeddings.dtype),
            like((8, wide), jnp.float32),
        ),
        in_specs=[VMEM] * (members + others - 1),
        out_specs=(VMEM,) * 4,
        scratch_shapes=facing_scratch,
        compiler_params=params(24),
        cost_estimate=cost,
        name="near",
    )(*own, *facing[:0:-1])
    total = pl.pallas_call(
        functools.partial(far_kernel, chunk, rate),
        out_shape=like((columns, wide), jnp.float32),
        in_specs=[VMEM] * (3 + others),
        out_specs=VMEM,
        scratch_shapes=facing_scratch,
        compiler_params=params(24),
        cost_estimate=cost,
        name="far",
    )(near_total, own_points, weights, *across[::-1])
    totals = [total] + swaps(total, own_masks)
    gram, sketched = pl.pallas_call(
        functools.partial(gram_kernel, members, near),
        out_shape=(
            like((columns, 2 * columns), jnp.float32),
            like((columns, count), jnp.float32),
        ),
        in_specs=[VMEM] * (members + 1),
        out_specs=(VMEM, VMEM),
        scratch_shapes=[
            pltpu.VMEM((columns, wide), jnp.float32),
            pltpu.VMEM((columns, wide), sketch.dtype),
        ],
        compiler_params=params(24),
        name="gram",
    )(*totals[::-1], own_tests)
    gram = gram + swap(gram, cols)
    mask = near
    grams = [gram]
    while mask < cols:
        grams = [tree(grams)]
        masks = [mask, 2 * mask, 3 * mask] if 2 * mask < cols else [mask]
        grams += swaps(grams[0], masks)
        mask *= len(masks) + 1
    scale = float(devices * count) ** 0.5

    def solve(grams, sketched):
        return pl.pallas_call(
            functools.partial(solve_kernel, scale),
            out_shape=(
                like((columns, count), jnp.float32),
                like((columns, count), jnp.float32),
                like((1, 1), jnp.float32),
            ),
            in_specs=[VMEM] * (len(grams) + 1),
            out_specs=(VMEM, VMEM, pl.BlockSpec(memory_space=pltpu.SMEM)),
            compiler_params=params(8),
            name="solve",
        )(*grams, sketched)

    def refine(first, basis):
        gram = pl.pallas_call(
            again_kernel,
            out_shape=like((columns, 2 * columns), jnp.float32),
            in_specs=[VMEM],
            out_specs=VMEM,
            compiler_params=params(8),
            name="again",
        )(first)
        mask = 1
        while mask < devices:
            gram = gram + swap(gram, mask)
            mask *= 2
        return solve([gram], first)[0]

    basis, first, margin = solve(grams[::-1], sketched)
    basis = lax.cond(margin[0, 0] > MARGIN, lambda first, basis: basis, refine, first, basis)
    return basis.T, first.T


def solution(mesh):
    placed = P(AXES, None)
    return jax.shard_map(
        functools.partial(per_device, rows=mesh.shape["row"], cols=mesh.shape["col"]),
        mesh=mesh,
        in_specs=(placed, placed),
        out_specs=(placed, placed),
        check_vma=False,
    )
```

```python
import functools

import jax
import jax.numpy as jnp
from jax import lax
from jax.experimental import pallas as pl
from jax.experimental.pallas import tpu as pltpu
from jax.sharding import PartitionSpec as P

AXES = ("row", "col")
NT = (((1,), (1,)), ((), ()))
NN = (((1,), (0,)), ((), ()))
LOG2E = 1.4426950408889634
MARGIN = 2.0**-7
VMEM = pl.BlockSpec(memory_space=pltpu.VMEM)
HBM = pl.BlockSpec(memory_space=pltpu.HBM)


def params(mebibytes):
    return pltpu.CompilerParams(vmem_limit_bytes=mebibytes << 20)


def tree(values):
    while len(values) > 1:
        values = [a + b for a, b in zip(values[::2], values[1::2])]
    return values[0]


def pack_kernel(points_ref, tests_ref, out_ref, sems):
    count, width = points_ref.shape
    pieces = width // count
    depth = tests_ref.shape[0] // pieces
    copies = [pltpu.make_async_copy(points_ref, out_ref.at[:count, :], sems.at[0])]
    for piece in range(pieces):
        copies.append(
            pltpu.make_async_copy(
                tests_ref.at[piece * depth : (piece + 1) * depth, :],
                out_ref.at[count:, piece * count : (piece + 1) * count],
                sems.at[piece + 1],
            )
        )
    for copy in copies:
        copy.start()
    for copy in copies:
        copy.wait()


def put_tests(pack, tests, at):
    height, width = pack.shape
    columns = tests.shape[0]
    count = height * width // (width + columns)
    pieces = width // count
    depth = columns // pieces
    for piece in range(pieces):
        tests[piece * depth : (piece + 1) * depth, at * count : (at + 1) * count] = pack[
            count:, piece * count : (piece + 1) * count
        ]


def weights_of(points, rate):
    wide = points.astype(jnp.float32)
    return jnp.sum(wide * wide, axis=1, keepdims=True) * rate


def accumulate(packs, total, own_ref, weights_ref, points, tests, chunk, rate):
    count = points.shape[0] // len(packs)
    for at, pack in enumerate(packs):
        points[at * count : (at + 1) * count, :] = pack[:count, :]
        put_tests(pack, tests, at)
    for start in range(0, len(packs) * count, chunk):
        block = points[start : start + chunk, :]
        cross = lax.dot_general(block, own_ref[...], NT, preferred_element_type=jnp.float32)
        power = cross * (2.0 * rate) - (weights_of(block, rate) + weights_ref[:1, :])
        tile = jnp.exp2(power).astype(jnp.bfloat16)
        part = lax.dot_general(
            tests[:, start : start + chunk], tile, NN, preferred_element_type=jnp.float32
        )
        total = part if total is None else total + part
    return total


def near_kernel(members, chunk, rate, *refs):
    total_ref, tests_ref, own_ref, weights_ref, points, tests = refs[-6:]
    packs = refs[:-6]
    count = own_ref.shape[0] // members
    for at in range(members):
        own_ref[at * count : (at + 1) * count, :] = packs[at][:count, :]
        put_tests(packs[at], tests_ref, at)
        column = weights_of(packs[at][:count, :], rate)
        weights_ref[:, at * count : (at + 1) * count] = jnp.broadcast_to(column, (count, count)).T[:8]
    facing = packs[:1] + packs[:members-1:-1]
    total_ref[...] = accumulate(facing, None, own_ref, weights_ref, points, tests, chunk, rate)


def far_kernel(chunk, rate, near_ref, own_ref, weights_ref, *refs):
    packs, (total_ref, points, tests) = refs[:-3], refs[-3:]
    total_ref[...] = accumulate(
        packs, near_ref[...], own_ref, weights_ref, points, tests, chunk, rate
    )


def products(tests, whole):
    parts = []
    rest = whole
    size = whole.shape[0]
    for _ in range(3):
        parts.append(rest.astype(jnp.bfloat16))
        rest = rest - parts[-1].astype(jnp.float32)
    core, gram = None, None
    for at in (2, 1, 0):
        stack = jnp.concatenate([tests] + parts[: 3 - at], axis=0)
        out = lax.dot_general(stack, parts[at], NT, preferred_element_type=jnp.float32)
        pieces = [out[size * p : size * (p + 1), :] for p in range(4 - at)]
        mirror = lax.dot_general(parts[at], tests, NT, preferred_element_type=jnp.float32)
        piece = pieces[0] + mirror
        core = piece if core is None else core + piece
        inner = pieces[-1]
        for piece in pieces[-2:0:-1]:
            inner = inner + piece
        gram = inner if gram is None else gram + inner
    return core * 0.5, (gram + gram.T) * 0.5


def again_kernel(first_ref, gram_ref):
    first = first_ref[...]
    _, gram = products(first.astype(jnp.bfloat16), first)
    gram_ref[...] = jnp.concatenate([gram, gram], axis=1)


def gram_kernel(members, near, *refs):
    totals, (tests_ref, gram_ref, sketched_ref, whole, tests) = refs[members - 1 :: -1], refs[members:]
    count = sketched_ref.shape[1]
    here = lax.axis_index("row") // 2 * near + lax.axis_index("col") % near
    for at in range(members):
        part = tree([
            totals[j][:, (at ^ j) * count : ((at ^ j) + 1) * count] for j in range(members)
        ])
        if at == 0:
            sketched_ref[...] = part
        place = pl.ds(pl.multiple_of((here ^ at) * count, count), count)
        whole[:, place] = part
        tests[:, place] = tests_ref[:, at * count : (at + 1) * count]
    core, gram = products(tests[...], whole[...])
    gram_ref[...] = jnp.concatenate([core, gram], axis=1)


def solve_kernel(scale, *refs):
    grams, (sketched_ref, basis_ref, first_ref, margin_ref) = refs[:-4], refs[-4:]
    both = tree([ref[...] for ref in grams[::-1]])
    size, rows = both.shape[0], 8
    count = size // rows
    sketched = sketched_ref[...]
    sides = [jnp.concatenate([sketched[:, at : at + size]] * 2, axis=1) for at in (0, size)]
    stacks = [[m[at : at + rows, :] for at in range(0, size, rows)] for m in [both] + sides]
    half = lax.broadcasted_iota(jnp.int32, (rows, 2 * size), 1) < size

    def spread(value):
        return jnp.broadcast_to(value, (rows, 2 * size))

    def column(value, at):
        left, right = value[:, at : at + 1], value[:, size + at : size + at + 1]
        return jnp.where(half, spread(left), spread(right))

    place = lax.broadcasted_iota(jnp.int32, (rows, 2 * size), 1)
    pivots = jnp.ones((rows, 2 * size), jnp.float32)
    outs = [[], []]
    for block in range(count):
        first_row = block * rows
        columns = [column(stacks[0][block], first_row + j) for j in range(rows)]
        part = [[spread(columns[j][m : m + 1, :]) for j in range(m + 1)] for m in range(rows)]
        lower = [[None] * rows for _ in range(rows)]
        inverse = []
        for j in range(rows):
            inverse.append(1.0 / part[j][j])
            for m in range(j + 1, rows):
                lower[m][j] = part[m][j] * inverse[j]
            for m in range(j + 1, rows):
                for q in range(j + 1, m + 1):
                    part[m][q] = part[m][q] - lower[m][j] * part[q][j]
        for j in range(rows):
            pivots = jnp.where(place == size + first_row + j, part[j][j], pivots)
        steps = []
        for stack in stacks:
            lines = [spread(stack[block][j : j + 1, :]) for j in range(rows)]
            for j in range(rows):
                for m in range(j + 1, rows):
                    lines[m] = lines[m] - lower[m][j] * lines[j]
            if steps:
                for j in range(rows):
                    root = lax.rsqrt(part[j][j]) * scale
                    outs[len(steps) - 1].append((lines[j] * root)[:1, :])
            lines = [line * r for line, r in zip(lines, inverse)]
            for j in range(rows - 1, 0, -1):
                for m in range(j):
                    lines[m] = lines[m] - lower[j][m] * lines[j]
            steps.append(lines)
        for below in range(block + 1, count):
            factors = [column(stacks[0][below], first_row + j) for j in range(rows)]
            for stack, lines in zip(stacks, steps):
                update = factors[0] * lines[0]
                for j in range(1, rows):
                    update = update + factors[j] * lines[j]
                stack[below] = stack[below] - update
    at_row = lax.broadcasted_iota(jnp.int32, both.shape, 0)
    at_lane = lax.broadcasted_iota(jnp.int32, both.shape, 1)
    diagonal = jnp.sum(jnp.where(at_lane == at_row + size, both, 0.0), axis=0, keepdims=True)
    kept = jnp.where(at_lane[:1] < size, 1.0, pivots[:1] / diagonal)
    margin_ref[0, 0] = jnp.min(kept)
    left, right = [jnp.concatenate(lines, axis=0) for lines in outs]
    first_ref[...] = jnp.concatenate([left[:, :size], right[:, :size]], axis=1)
    basis_ref[...] = jnp.concatenate([left[:, size:], right[:, size:]], axis=1)


def per_device(embeddings, sketch, rows, cols):
    count, width = embeddings.shape
    columns = sketch.shape[1]
    rate = 3.0 / width * LOG2E
    near = 2 if cols % 2 == 0 else 1
    members, others = rows // 2 * near, cols // near
    devices = rows * cols
    like = jax.ShapeDtypeStruct
    stay = pltpu.with_memory_space_constraint
    wide, chunk = members * count, 512

    def swap(value, mask):
        return lax.ppermute(value, AXES, [(i, i ^ mask) for i in range(devices)])

    def swaps(value, masks):
        return [swap(value, mask) for mask in masks]

    packed = pl.pallas_call(
        pack_kernel,
        out_shape=like((count + columns * count // width, width), embeddings.dtype),
        in_specs=[HBM, HBM],
        out_specs=VMEM,
        scratch_shapes=[pltpu.SemaphoreType.DMA((1 + width // count,))],
        compiler_params=params(4),
        name="pack",
    )(stay(embeddings, pltpu.HBM), stay(sketch.T, pltpu.HBM))
    own_masks = [2 * cols * x + l for x in range(rows // 2) for l in range(near)][1:]
    far_masks = [near * j for j in range(1, others)]
    facing = [packed] + swaps(packed, far_masks)
    own = [packed] + swaps(packed, own_masks)
    across = [swap(block, cols) for block in facing]
    early, late = facing + across[:1] + across[-1:], across[1:-1]

    def scratch(blocks):
        return [
            pltpu.VMEM((len(blocks) * count, width), embeddings.dtype),
            pltpu.VMEM((columns, len(blocks) * count), sketch.dtype),
        ]

    def cost(blocks):
        deep = len(blocks) * count
        return pl.CostEstimate(
            flops=2 * wide * deep * (width + columns),
            bytes_accessed=2 * (wide + deep) * width,
            transcendentals=wide * deep,
        )

    near_total, own_tests, own_points, weights = pl.pallas_call(
        functools.partial(near_kernel, members, chunk, rate),
        out_shape=(
            like((columns, wide), jnp.float32),
            like((columns, wide), sketch.dtype),
            like((wide, width), embeddings.dtype),
            like((8, wide), jnp.float32),
        ),
        in_specs=[VMEM] * (members + len(early) - 1),
        out_specs=(VMEM,) * 4,
        scratch_shapes=scratch(early),
        compiler_params=params(24),
        cost_estimate=cost(early),
        name="near",
    )(*own, *early[:0:-1])
    total = pl.pallas_call(
        functools.partial(far_kernel, chunk, rate),
        out_shape=like((columns, wide), jnp.float32),
        in_specs=[VMEM] * (3 + len(late)),
        out_specs=VMEM,
        scratch_shapes=scratch(late),
        compiler_params=params(24),
        cost_estimate=cost(late),
        name="far",
    )(near_total, own_points, weights, *late[::-1])
    totals = [total] + swaps(total, own_masks)
    gram, sketched = pl.pallas_call(
        functools.partial(gram_kernel, members, near),
        out_shape=(
            like((columns, 2 * columns), jnp.float32),
            like((columns, count), jnp.float32),
        ),
        in_specs=[VMEM] * (members + 1),
        out_specs=(VMEM, VMEM),
        scratch_shapes=[
            pltpu.VMEM((columns, wide), jnp.float32),
            pltpu.VMEM((columns, wide), sketch.dtype),
        ],
        compiler_params=params(24),
        name="gram",
    )(*totals[::-1], own_tests)
    gram = gram + swap(gram, cols)
    mask = near
    grams = [gram]
    while mask < cols:
        grams = [tree(grams)]
        masks = [mask, 2 * mask, 3 * mask] if 2 * mask < cols else [mask]
        grams += swaps(grams[0], masks)
        mask *= len(masks) + 1
    scale = float(devices * count) ** 0.5

    def solve(grams, sketched):
        return pl.pallas_call(
            functools.partial(solve_kernel, scale),
            out_shape=(
                like((columns, count), jnp.float32),
                like((columns, count), jnp.float32),
                like((1, 1), jnp.float32),
            ),
            in_specs=[VMEM] * (len(grams) + 1),
            out_specs=(VMEM, VMEM, pl.BlockSpec(memory_space=pltpu.SMEM)),
            compiler_params=params(8),
            name="solve",
        )(*grams, sketched)

    def refine(first, basis):
        gram = pl.pallas_call(
            again_kernel,
            out_shape=like((columns, 2 * columns), jnp.float32),
            in_specs=[VMEM],
            out_specs=VMEM,
            compiler_params=params(8),
            name="again",
        )(first)
        mask = 1
        while mask < devices:
            gram = gram + swap(gram, mask)
            mask *= 2
        return solve([gram], first)[0]

    basis, first, margin = solve(grams[::-1], sketched)
    basis = lax.cond(margin[0, 0] > MARGIN, lambda first, basis: basis, refine, first, basis)
    return basis.T, first.T


def solution(mesh):
    placed = P(AXES, None)
    return jax.shard_map(
        functools.partial(per_device, rows=mesh.shape["row"], cols=mesh.shape["col"]),
        mesh=mesh,
        in_specs=(placed, placed),
        out_specs=(placed, placed),
        check_vma=False,
    )
```

```python
import functools

import jax
import jax.numpy as jnp
from jax import lax
from jax.experimental import pallas as pl
from jax.experimental.pallas import tpu as pltpu
from jax.sharding import PartitionSpec as P

AXES = ("row", "col")
NT = (((1,), (1,)), ((), ()))
NN = (((1,), (0,)), ((), ()))
LOG2E = 1.4426950408889634
MARGIN = 2.0**-7
VMEM = pl.BlockSpec(memory_space=pltpu.VMEM)
HBM = pl.BlockSpec(memory_space=pltpu.HBM)


def params(mebibytes):
    return pltpu.CompilerParams(vmem_limit_bytes=mebibytes << 20)


def tree(values):
    while len(values) > 1:
        values = [a + b for a, b in zip(values[::2], values[1::2])]
    return values[0]


def pack_kernel(points_ref, tests_ref, out_ref, sems):
    count, width = points_ref.shape
    pieces = width // count
    depth = tests_ref.shape[0] // pieces
    copies = [pltpu.make_async_copy(points_ref, out_ref.at[:count, :], sems.at[0])]
    for piece in range(pieces):
        copies.append(
            pltpu.make_async_copy(
                tests_ref.at[piece * depth : (piece + 1) * depth, :],
                out_ref.at[count:, piece * count : (piece + 1) * count],
                sems.at[piece + 1],
            )
        )
    for copy in copies:
        copy.start()
    for copy in copies:
        copy.wait()


def put_tests(pack, tests, at):
    height, width = pack.shape
    columns = tests.shape[0]
    count = height * width // (width + columns)
    pieces = width // count
    depth = columns // pieces
    for piece in range(pieces):
        tests[piece * depth : (piece + 1) * depth, at * count : (at + 1) * count] = pack[
            count:, piece * count : (piece + 1) * count
        ]


def weights_of(points, rate):
    wide = points.astype(jnp.float32)
    return jnp.sum(wide * wide, axis=1, keepdims=True) * rate


def accumulate(packs, total, own_ref, weights_ref, points, tests, chunk, rate):
    count = points.shape[0] // len(packs)
    for at, pack in enumerate(packs):
        points[at * count : (at + 1) * count, :] = pack[:count, :]
        put_tests(pack, tests, at)
    for start in range(0, len(packs) * count, chunk):
        block = points[start : start + chunk, :]
        cross = lax.dot_general(block, own_ref[...], NT, preferred_element_type=jnp.float32)
        power = cross * (2.0 * rate) - (weights_of(block, rate) + weights_ref[:1, :])
        tile = jnp.exp2(power).astype(jnp.bfloat16)
        part = lax.dot_general(
            tests[:, start : start + chunk], tile, NN, preferred_element_type=jnp.float32
        )
        total = part if total is None else total + part
    return total


def near_kernel(members, chunk, rate, *refs):
    total_ref, tests_ref, own_ref, weights_ref, points, tests = refs[-6:]
    packs = refs[:-6]
    count = own_ref.shape[0] // members
    for at in range(members):
        own_ref[at * count : (at + 1) * count, :] = packs[at][:count, :]
        put_tests(packs[at], tests_ref, at)
        column = weights_of(packs[at][:count, :], rate)
        weights_ref[:, at * count : (at + 1) * count] = jnp.broadcast_to(column, (count, count)).T[:8]
    facing = packs[:1] + packs[:members-1:-1]
    total_ref[...] = accumulate(facing, None, own_ref, weights_ref, points, tests, chunk, rate)


def far_kernel(chunk, rate, near_ref, own_ref, weights_ref, *refs):
    packs, (total_ref, points, tests) = refs[:-3], refs[-3:]
    total_ref[...] = accumulate(
        packs, near_ref[...], own_ref, weights_ref, points, tests, chunk, rate
    )


def products(tests, whole):
    parts = []
    rest = whole
    size = whole.shape[0]
    for _ in range(3):
        parts.append(rest.astype(jnp.bfloat16))
        rest = rest - parts[-1].astype(jnp.float32)
    core, gram = None, None
    for at in (2, 1, 0):
        stack = jnp.concatenate([tests] + parts[: 3 - at], axis=0)
        out = lax.dot_general(stack, parts[at], NT, preferred_element_type=jnp.float32)
        pieces = [out[size * p : size * (p + 1), :] for p in range(4 - at)]
        mirror = lax.dot_general(parts[at], tests, NT, preferred_element_type=jnp.float32)
        piece = pieces[0] + mirror
        core = piece if core is None else core + piece
        inner = pieces[-1]
        for piece in pieces[-2:0:-1]:
            inner = inner + piece
        gram = inner if gram is None else gram + inner
    return core * 0.5, (gram + gram.T) * 0.5


def again_kernel(first_ref, gram_ref):
    first = first_ref[...]
    _, gram = products(first.astype(jnp.bfloat16), first)
    gram_ref[...] = jnp.concatenate([gram, gram], axis=1)


def gram_kernel(members, near, *refs):
    totals, (tests_ref, gram_ref, sketched_ref, whole, tests) = refs[members - 1 :: -1], refs[members:]
    count = sketched_ref.shape[1]
    here = lax.axis_index("row") // 2 * near + lax.axis_index("col") % near
    for at in range(members):
        part = tree([
            totals[j][:, (at ^ j) * count : ((at ^ j) + 1) * count] for j in range(members)
        ])
        if at == 0:
            sketched_ref[...] = part
        place = pl.ds(pl.multiple_of((here ^ at) * count, count), count)
        whole[:, place] = part
        tests[:, place] = tests_ref[:, at * count : (at + 1) * count]
    core, gram = products(tests[...], whole[...])
    gram_ref[...] = jnp.concatenate([core, gram], axis=1)


def solve_kernel(scale, *refs):
    grams, (sketched_ref, basis_ref, first_ref, margin_ref) = refs[:-4], refs[-4:]
    both = tree([ref[...] for ref in grams[::-1]])
    size, rows = both.shape[0], 8
    count = size // rows
    sketched = sketched_ref[...]
    sides = [jnp.concatenate([sketched[:, at : at + size]] * 2, axis=1) for at in (0, size)]
    stacks = [[m[at : at + rows, :] for at in range(0, size, rows)] for m in [both] + sides]
    half = lax.broadcasted_iota(jnp.int32, (rows, 2 * size), 1) < size

    def spread(value):
        return jnp.broadcast_to(value, (rows, 2 * size))

    def column(value, at):
        left, right = value[:, at : at + 1], value[:, size + at : size + at + 1]
        return jnp.where(half, spread(left), spread(right))

    place = lax.broadcasted_iota(jnp.int32, (rows, 2 * size), 1)
    pivots = jnp.ones((rows, 2 * size), jnp.float32)
    outs = [[], []]
    for block in range(count):
        first_row = block * rows
        after = range(block + 1, count)
        columns = [column(stacks[0][block], first_row + j) for j in range(rows)]
        part = [[spread(columns[j][m : m + 1, :]) for j in range(m + 1)] for m in range(rows)]
        below = {b: [column(stacks[0][b], first_row + j) for j in range(rows)] for b in after}
        lines = [[spread(stack[block][j : j + 1, :]) for j in range(rows)] for stack in stacks]
        for j in range(rows):
            pivot = part[j][j]
            ahead = part[j + 1][j] * part[j + 1][j] if j + 1 < rows else None
            inverse = 1.0 / pivot
            pivots = jnp.where(place == size + first_row + j, pivot, pivots)
            for side, line in zip(outs, lines[1:]):
                side.append((line[j] * (lax.rsqrt(pivot) * scale))[:1, :])
            rest = range(j + 1, rows)
            factors = {m: part[m][j] * inverse for m in rest}
            for m in rest:
                for q in range(j + 1, m + 1):
                    lost = ahead * inverse if m == j + 1 else factors[m] * part[q][j]
                    part[m][q] = part[m][q] - lost
            for b in after:
                factor = below[b][j] * inverse
                for m in rest:
                    below[b][m] = below[b][m] - factor * part[m][j]
                for stack, line in zip(stacks, lines):
                    stack[b] = stack[b] - factor * line[j]
            for line in lines:
                for m in rest:
                    line[m] = line[m] - factors[m] * line[j]
    at_row = lax.broadcasted_iota(jnp.int32, both.shape, 0)
    at_lane = lax.broadcasted_iota(jnp.int32, both.shape, 1)
    diagonal = jnp.sum(jnp.where(at_lane == at_row + size, both, 0.0), axis=0, keepdims=True)
    kept = jnp.where(at_lane[:1] < size, 1.0, pivots[:1] / diagonal)
    margin_ref[0, 0] = jnp.min(kept)
    left, right = [jnp.concatenate(lines, axis=0) for lines in outs]
    first_ref[...] = jnp.concatenate([left[:, :size], right[:, :size]], axis=1)
    basis_ref[...] = jnp.concatenate([left[:, size:], right[:, size:]], axis=1)


def per_device(embeddings, sketch, rows, cols):
    count, width = embeddings.shape
    columns = sketch.shape[1]
    rate = 3.0 / width * LOG2E
    near = 2 if cols % 2 == 0 else 1
    members, others = rows // 2 * near, cols // near
    devices = rows * cols
    like = jax.ShapeDtypeStruct
    stay = pltpu.with_memory_space_constraint
    wide, chunk = members * count, 512

    def swap(value, mask):
        return lax.ppermute(value, AXES, [(i, i ^ mask) for i in range(devices)])

    def swaps(value, masks):
        return [swap(value, mask) for mask in masks]

    packed = pl.pallas_call(
        pack_kernel,
        out_shape=like((count + columns * count // width, width), embeddings.dtype),
        in_specs=[HBM, HBM],
        out_specs=VMEM,
        scratch_shapes=[pltpu.SemaphoreType.DMA((1 + width // count,))],
        compiler_params=params(4),
        name="pack",
    )(stay(embeddings, pltpu.HBM), stay(sketch.T, pltpu.HBM))
    own_masks = [2 * cols * x + l for x in range(rows // 2) for l in range(near)][1:]
    far_masks = [near * j for j in range(1, others)]
    facing = [packed] + swaps(packed, far_masks)
    own = [packed] + swaps(packed, own_masks)
    across = [swap(block, cols) for block in facing]
    early, late = facing + across[:1] + across[-1:], across[1:-1]

    def scratch(blocks):
        return [
            pltpu.VMEM((len(blocks) * count, width), embeddings.dtype),
            pltpu.VMEM((columns, len(blocks) * count), sketch.dtype),
        ]

    def cost(blocks):
        deep = len(blocks) * count
        return pl.CostEstimate(
            flops=2 * wide * deep * (width + columns),
            bytes_accessed=2 * (wide + deep) * width,
            transcendentals=wide * deep,
        )

    near_total, own_tests, own_points, weights = pl.pallas_call(
        functools.partial(near_kernel, members, chunk, rate),
        out_shape=(
            like((columns, wide), jnp.float32),
            like((columns, wide), sketch.dtype),
            like((wide, width), embeddings.dtype),
            like((8, wide), jnp.float32),
        ),
        in_specs=[VMEM] * (members + len(early) - 1),
        out_specs=(VMEM,) * 4,
        scratch_shapes=scratch(early),
        compiler_params=params(24),
        cost_estimate=cost(early),
        name="near",
    )(*own, *early[:0:-1])
    total = pl.pallas_call(
        functools.partial(far_kernel, chunk, rate),
        out_shape=like((columns, wide), jnp.float32),
        in_specs=[VMEM] * (3 + len(late)),
        out_specs=VMEM,
        scratch_shapes=scratch(late),
        compiler_params=params(24),
        cost_estimate=cost(late),
        name="far",
    )(near_total, own_points, weights, *late[::-1])
    totals = [total] + swaps(total, own_masks)
    gram, sketched = pl.pallas_call(
        functools.partial(gram_kernel, members, near),
        out_shape=(
            like((columns, 2 * columns), jnp.float32),
            like((columns, count), jnp.float32),
        ),
        in_specs=[VMEM] * (members + 1),
        out_specs=(VMEM, VMEM),
        scratch_shapes=[
            pltpu.VMEM((columns, wide), jnp.float32),
            pltpu.VMEM((columns, wide), sketch.dtype),
        ],
        compiler_params=params(24),
        name="gram",
    )(*totals[::-1], own_tests)
    gram = gram + swap(gram, cols)
    mask = near
    grams = [gram]
    while mask < cols:
        grams = [tree(grams)]
        masks = [mask, 2 * mask, 3 * mask] if 2 * mask < cols else [mask]
        grams += swaps(grams[0], masks)
        mask *= len(masks) + 1
    scale = float(devices * count) ** 0.5

    def solve(grams, sketched):
        return pl.pallas_call(
            functools.partial(solve_kernel, scale),
            out_shape=(
                like((columns, count), jnp.float32),
                like((columns, count), jnp.float32),
                like((1, 1), jnp.float32),
            ),
            in_specs=[VMEM] * (len(grams) + 1),
            out_specs=(VMEM, VMEM, pl.BlockSpec(memory_space=pltpu.SMEM)),
            compiler_params=params(8),
            name="solve",
        )(*grams, sketched)

    def refine(first, basis):
        gram = pl.pallas_call(
            again_kernel,
            out_shape=like((columns, 2 * columns), jnp.float32),
            in_specs=[VMEM],
            out_specs=VMEM,
            compiler_params=params(8),
            name="again",
        )(first)
        mask = 1
        while mask < devices:
            gram = gram + swap(gram, mask)
            mask *= 2
        return solve([gram], first)[0]

    basis, first, margin = solve(grams[::-1], sketched)
    basis = lax.cond(margin[0, 0] > MARGIN, lambda first, basis: basis, refine, first, basis)
    return basis.T, first.T


def solution(mesh):
    placed = P(AXES, None)
    return jax.shard_map(
        functools.partial(per_device, rows=mesh.shape["row"], cols=mesh.shape["col"]),
        mesh=mesh,
        in_specs=(placed, placed),
        out_specs=(placed, placed),
        check_vma=False,
    )
```

```python
import functools

import jax
import jax.numpy as jnp
from jax import lax
from jax.experimental import pallas as pl
from jax.experimental.pallas import tpu as pltpu
from jax.sharding import PartitionSpec as P

AXES = ("row", "col")
NT = (((1,), (1,)), ((), ()))
NN = (((1,), (0,)), ((), ()))
LOG2E = 1.4426950408889634
MARGIN = 2.0**-7
VMEM = pl.BlockSpec(memory_space=pltpu.VMEM)
HBM = pl.BlockSpec(memory_space=pltpu.HBM)


def params(mebibytes):
    return pltpu.CompilerParams(vmem_limit_bytes=mebibytes << 20)


def tree(values):
    while len(values) > 1:
        values = [a + b for a, b in zip(values[::2], values[1::2])]
    return values[0]


def pack_kernel(points_ref, tests_ref, out_ref, sems):
    count, width = points_ref.shape
    pieces = width // count
    depth = tests_ref.shape[0] // pieces
    copies = [pltpu.make_async_copy(points_ref, out_ref.at[:count, :], sems.at[0])]
    for piece in range(pieces):
        copies.append(
            pltpu.make_async_copy(
                tests_ref.at[piece * depth : (piece + 1) * depth, :],
                out_ref.at[count:, piece * count : (piece + 1) * count],
                sems.at[piece + 1],
            )
        )
    for copy in copies:
        copy.start()
    for copy in copies:
        copy.wait()


def put_tests(pack, tests, at):
    height, width = pack.shape
    columns = tests.shape[0]
    count = height * width // (width + columns)
    pieces = width // count
    depth = columns // pieces
    for piece in range(pieces):
        tests[piece * depth : (piece + 1) * depth, at * count : (at + 1) * count] = pack[
            count:, piece * count : (piece + 1) * count
        ]


def weights_of(points, rate):
    wide = points.astype(jnp.float32)
    return jnp.sum(wide * wide, axis=1, keepdims=True) * rate


def accumulate(packs, total, own_ref, weights_ref, points, tests, chunk, rate):
    count = points.shape[0] // len(packs)
    for at, pack in enumerate(packs):
        points[at * count : (at + 1) * count, :] = pack[:count, :]
        put_tests(pack, tests, at)
    for start in range(0, len(packs) * count, chunk):
        block = points[start : start + chunk, :]
        cross = lax.dot_general(block, own_ref[...], NT, preferred_element_type=jnp.float32)
        power = cross * (2.0 * rate) - (weights_of(block, rate) + weights_ref[:1, :])
        tile = jnp.exp2(power).astype(jnp.bfloat16)
        part = lax.dot_general(
            tests[:, start : start + chunk], tile, NN, preferred_element_type=jnp.float32
        )
        total = part if total is None else total + part
    return total


def near_kernel(members, chunk, rate, *refs):
    total_ref, tests_ref, own_ref, weights_ref, points, tests = refs[-6:]
    packs = refs[:-6]
    count = own_ref.shape[0] // members
    for at in range(members):
        own_ref[at * count : (at + 1) * count, :] = packs[at][:count, :]
        put_tests(packs[at], tests_ref, at)
        column = weights_of(packs[at][:count, :], rate)
        weights_ref[:, at * count : (at + 1) * count] = jnp.broadcast_to(column, (count, count)).T[:8]
    facing = packs[:1] + packs[:members-1:-1]
    total_ref[...] = accumulate(facing, None, own_ref, weights_ref, points, tests, chunk, rate)


def far_kernel(chunk, rate, near_ref, own_ref, weights_ref, *refs):
    packs, (total_ref, points, tests) = refs[:-3], refs[-3:]
    total_ref[...] = accumulate(
        packs, near_ref[...], own_ref, weights_ref, points, tests, chunk, rate
    )


def products(tests, whole):
    parts = []
    rest = whole
    size = whole.shape[0]
    for _ in range(3):
        parts.append(rest.astype(jnp.bfloat16))
        rest = rest - parts[-1].astype(jnp.float32)
    core, gram = None, None
    for at in (2, 1, 0):
        stack = jnp.concatenate([tests] + parts[: 3 - at], axis=0)
        out = lax.dot_general(stack, parts[at], NT, preferred_element_type=jnp.float32)
        pieces = [out[size * p : size * (p + 1), :] for p in range(4 - at)]
        mirror = lax.dot_general(parts[at], tests, NT, preferred_element_type=jnp.float32)
        piece = pieces[0] + mirror
        core = piece if core is None else core + piece
        inner = pieces[-1]
        for piece in pieces[-2:0:-1]:
            inner = inner + piece
        gram = inner if gram is None else gram + inner
    return core * 0.5, (gram + gram.T) * 0.5


def again_kernel(first_ref, gram_ref):
    first = first_ref[...]
    _, gram = products(first.astype(jnp.bfloat16), first)
    gram_ref[...] = jnp.concatenate([gram, gram], axis=1)


def gram_kernel(members, near, *refs):
    totals, (tests_ref, gram_ref, sketched_ref, whole, tests) = refs[members - 1 :: -1], refs[members:]
    count = sketched_ref.shape[1]
    here = lax.axis_index("row") // 2 * near + lax.axis_index("col") % near
    for at in range(members):
        part = tree([
            totals[j][:, (at ^ j) * count : ((at ^ j) + 1) * count] for j in range(members)
        ])
        if at == 0:
            sketched_ref[...] = part
        place = pl.ds(pl.multiple_of((here ^ at) * count, count), count)
        whole[:, place] = part
        tests[:, place] = tests_ref[:, at * count : (at + 1) * count]
    core, gram = products(tests[...], whole[...])
    gram_ref[...] = jnp.concatenate([core, gram], axis=1)


def solve_kernel(scale, *refs):
    grams, (sketched_ref, basis_ref, first_ref, margin_ref) = refs[:-4], refs[-4:]
    both = tree([ref[...] for ref in grams[::-1]])
    size, rows = both.shape[0], 8
    count = size // rows
    sketched = sketched_ref[...]
    sides = [jnp.concatenate([sketched[:, at : at + size]] * 2, axis=1) for at in (0, size)]
    stacks = [[m[at : at + rows, :] for at in range(0, size, rows)] for m in [both] + sides]
    half = lax.broadcasted_iota(jnp.int32, (rows, 2 * size), 1) < size

    def spread(value):
        return jnp.broadcast_to(value, (rows, 2 * size))

    def column(value, at):
        left, right = value[:, at : at + 1], value[:, size + at : size + at + 1]
        return jnp.where(half, spread(left), spread(right))

    place = lax.broadcasted_iota(jnp.int32, (rows, 2 * size), 1)
    pivots = jnp.ones((rows, 2 * size), jnp.float32)
    outs = [[], []]
    for block in range(count):
        first_row = block * rows
        after = range(block + 1, count)
        columns = [column(stacks[0][block], first_row + j) for j in range(rows)]
        part = [[spread(columns[j][m : m + 1, :]) for j in range(m + 1)] for m in range(rows)]
        below = {b: [column(stacks[0][b], first_row + j) for j in range(rows)] for b in after}
        lines = [[spread(stack[block][j : j + 1, :]) for j in range(rows)] for stack in stacks]
        for j in range(rows):
            pivot = part[j][j]
            ahead = part[j + 1][j] * part[j + 1][j] if j + 1 < rows else None
            inverse = 1.0 / pivot
            pivots = jnp.where(place == size + first_row + j, pivot, pivots)
            for side, line in zip(outs, lines[1:]):
                side.append((line[j] * (lax.rsqrt(pivot) * scale))[:1, :])
            rest = range(j + 1, rows)
            factors = {m: part[m][j] * inverse for m in rest}
            for m in rest:
                for q in range(j + 1, m + 1):
                    lost = ahead * inverse if m == j + 1 else factors[m] * part[q][j]
                    part[m][q] = part[m][q] - lost
            for b in after:
                factor = below[b][j] * inverse
                for m in rest:
                    below[b][m] = below[b][m] - factor * part[m][j]
                for stack, line in zip(stacks, lines):
                    stack[b] = stack[b] - factor * line[j]
            for line in lines:
                for m in rest:
                    line[m] = line[m] - factors[m] * line[j]
    at_row = lax.broadcasted_iota(jnp.int32, both.shape, 0)
    at_lane = lax.broadcasted_iota(jnp.int32, both.shape, 1)
    diagonal = jnp.sum(jnp.where(at_lane == at_row + size, both, 0.0), axis=0, keepdims=True)
    kept = jnp.where(at_lane[:1] < size, 1.0, pivots[:1] / diagonal)
    margin_ref[0, 0] = jnp.min(kept)
    left, right = [jnp.concatenate(lines, axis=0) for lines in outs]
    first_ref[...] = jnp.concatenate([left[:, :size], right[:, :size]], axis=1)
    basis_ref[...] = jnp.concatenate([left[:, size:], right[:, size:]], axis=1)


def per_device(embeddings, sketch, rows, cols):
    count, width = embeddings.shape
    columns = sketch.shape[1]
    rate = 3.0 / width * LOG2E
    near = 2 if cols % 2 == 0 else 1
    members, others = rows // 2 * near, cols // near
    devices = rows * cols
    like = jax.ShapeDtypeStruct
    stay = pltpu.with_memory_space_constraint
    wide, chunk = members * count, 512

    def swap(value, mask):
        return lax.ppermute(value, AXES, [(i, i ^ mask) for i in range(devices)])

    def swaps(value, masks):
        return [swap(value, mask) for mask in masks]

    packed = pl.pallas_call(
        pack_kernel,
        out_shape=like((count + columns * count // width, width), embeddings.dtype),
        in_specs=[HBM, HBM],
        out_specs=VMEM,
        scratch_shapes=[pltpu.SemaphoreType.DMA((1 + width // count,))],
        compiler_params=params(4),
        name="pack",
    )(stay(embeddings, pltpu.HBM), stay(sketch.T, pltpu.HBM))
    own_masks = [2 * cols * x + l for x in range(rows // 2) for l in range(near)][1:]
    far_masks = [near * j for j in range(1, others)]
    facing = [packed] + swaps(packed, far_masks)
    own = [packed] + swaps(packed, own_masks)
    across = [swap(block, cols) for block in facing]
    early, late = facing + across[:1] + across[-1:], across[1:-1]

    def scratch(blocks):
        return [
            pltpu.VMEM((len(blocks) * count, width), embeddings.dtype),
            pltpu.VMEM((columns, len(blocks) * count), sketch.dtype),
        ]

    def cost(blocks):
        deep = len(blocks) * count
        return pl.CostEstimate(
            flops=2 * wide * deep * (width + columns),
            bytes_accessed=2 * (wide + deep) * width,
            transcendentals=wide * deep,
        )

    near_total, own_tests, own_points, weights = pl.pallas_call(
        functools.partial(near_kernel, members, chunk, rate),
        out_shape=(
            like((columns, wide), jnp.float32),
            like((columns, wide), sketch.dtype),
            like((wide, width), embeddings.dtype),
            like((8, wide), jnp.float32),
        ),
        in_specs=[VMEM] * (members + len(early) - 1),
        out_specs=(VMEM,) * 4,
        scratch_shapes=scratch(early),
        compiler_params=params(24),
        cost_estimate=cost(early),
        name="near",
    )(*own, *early[:0:-1])
    total = pl.pallas_call(
        functools.partial(far_kernel, chunk, rate),
        out_shape=like((columns, wide), jnp.float32),
        in_specs=[VMEM] * (3 + len(late)),
        out_specs=VMEM,
        scratch_shapes=scratch(late),
        compiler_params=params(24),
        cost_estimate=cost(late),
        name="far",
    )(near_total, own_points, weights, *late[::-1])
    totals = [total] + swaps(total, own_masks)
    gram, sketched = pl.pallas_call(
        functools.partial(gram_kernel, members, near),
        out_shape=(
            like((columns, 2 * columns), jnp.float32),
            like((columns, count), jnp.float32),
        ),
        in_specs=[VMEM] * (members + 1),
        out_specs=(VMEM, VMEM),
        scratch_shapes=[
            pltpu.VMEM((columns, wide), jnp.float32),
            pltpu.VMEM((columns, wide), sketch.dtype),
        ],
        compiler_params=params(24),
        name="gram",
    )(*totals[::-1], own_tests)
    gram = gram + swap(gram, cols)
    mask = near
    grams = [gram]
    while mask < cols:
        grams = [tree(grams)]
        masks = [mask, 2 * mask, 3 * mask] if 2 * mask < cols else [mask]
        grams += swaps(grams[0], masks)
        mask *= len(masks) + 1
    scale = float(devices * count) ** 0.5

    def solve(grams, sketched):
        return pl.pallas_call(
            functools.partial(solve_kernel, scale),
            out_shape=(
                like((columns, count), jnp.float32),
                like((columns, count), jnp.float32),
                pltpu.SMEM((1, 1), jnp.float32),
            ),
            in_specs=[VMEM] * (len(grams) + 1),
            out_specs=(VMEM, VMEM, pl.BlockSpec(memory_space=pltpu.SMEM)),
            compiler_params=params(8),
            name="solve",
        )(*grams, sketched)

    def refine(first, basis):
        gram = pl.pallas_call(
            again_kernel,
            out_shape=like((columns, 2 * columns), jnp.float32),
            in_specs=[VMEM],
            out_specs=VMEM,
            compiler_params=params(8),
            name="again",
        )(first)
        mask = 1
        while mask < devices:
            gram = gram + swap(gram, mask)
            mask *= 2
        return solve([gram], first)[0]

    basis, first, margin = solve(grams[::-1], sketched)
    basis = lax.cond(margin[0, 0] > MARGIN, lambda first, basis: basis, refine, first, basis)
    return basis.T, first.T


def solution(mesh):
    placed = P(AXES, None)
    return jax.shard_map(
        functools.partial(per_device, rows=mesh.shape["row"], cols=mesh.shape["col"]),
        mesh=mesh,
        in_specs=(placed, placed),
        out_specs=(placed, placed),
        check_vma=False,
    )
```

```python
import functools

import jax
import jax.numpy as jnp
from jax import lax
from jax.experimental import pallas as pl
from jax.experimental.pallas import tpu as pltpu
from jax.sharding import PartitionSpec as P

AXES = ("row", "col")
NT = (((1,), (1,)), ((), ()))
NN = (((1,), (0,)), ((), ()))
LOG2E = 1.4426950408889634
MARGIN = 2.0**-7
VMEM = pl.BlockSpec(memory_space=pltpu.VMEM)
HBM = pl.BlockSpec(memory_space=pltpu.HBM)


def params(mebibytes):
    return pltpu.CompilerParams(vmem_limit_bytes=mebibytes << 20)


def tree(values):
    while len(values) > 1:
        values = [a + b for a, b in zip(values[::2], values[1::2])]
    return values[0]


def pack_kernel(points_ref, tests_ref, out_ref, sems):
    count, width = points_ref.shape
    pieces = width // count
    depth = tests_ref.shape[0] // pieces
    copies = [pltpu.make_async_copy(points_ref, out_ref.at[:count, :], sems.at[0])]
    for piece in range(pieces):
        copies.append(
            pltpu.make_async_copy(
                tests_ref.at[piece * depth : (piece + 1) * depth, :],
                out_ref.at[count:, piece * count : (piece + 1) * count],
                sems.at[piece + 1],
            )
        )
    for copy in copies:
        copy.start()
    for copy in copies:
        copy.wait()


def put_tests(pack, tests, at):
    height, width = pack.shape
    columns = tests.shape[0]
    count = height * width // (width + columns)
    pieces = width // count
    depth = columns // pieces
    for piece in range(pieces):
        tests[piece * depth : (piece + 1) * depth, at * count : (at + 1) * count] = pack[
            count:, piece * count : (piece + 1) * count
        ]


def weights_of(points, rate):
    wide = points.astype(jnp.float32)
    return jnp.sum(wide * wide, axis=1, keepdims=True) * rate


def accumulate(packs, total, own_ref, weights_ref, points, tests, chunk, rate):
    count = points.shape[0] // len(packs)
    for at, pack in enumerate(packs):
        points[at * count : (at + 1) * count, :] = pack[:count, :]
        put_tests(pack, tests, at)
    for start in range(0, len(packs) * count, chunk):
        block = points[start : start + chunk, :]
        cross = lax.dot_general(block, own_ref[...], NT, preferred_element_type=jnp.float32)
        power = cross * (2.0 * rate) - (weights_of(block, rate) + weights_ref[:1, :])
        tile = jnp.exp2(power).astype(jnp.bfloat16)
        part = lax.dot_general(
            tests[:, start : start + chunk], tile, NN, preferred_element_type=jnp.float32
        )
        total = part if total is None else total + part
    return total


def near_kernel(members, chunk, rate, *refs):
    total_ref, tests_ref, own_ref, weights_ref, points, tests = refs[-6:]
    packs = refs[:-6]
    count = own_ref.shape[0] // members
    for at in range(members):
        own_ref[at * count : (at + 1) * count, :] = packs[at][:count, :]
        put_tests(packs[at], tests_ref, at)
        column = weights_of(packs[at][:count, :], rate)
        weights_ref[:, at * count : (at + 1) * count] = jnp.broadcast_to(column, (count, count)).T[:8]
    facing = packs[:1] + packs[:members-1:-1]
    total_ref[...] = accumulate(facing, None, own_ref, weights_ref, points, tests, chunk, rate)


def far_kernel(chunk, rate, near_ref, own_ref, weights_ref, *refs):
    packs, (total_ref, points, tests) = refs[:-3], refs[-3:]
    total_ref[...] = accumulate(
        packs, near_ref[...], own_ref, weights_ref, points, tests, chunk, rate
    )


def products(tests, whole):
    parts = []
    rest = whole
    size = whole.shape[0]
    for _ in range(3):
        parts.append(rest.astype(jnp.bfloat16))
        rest = rest - parts[-1].astype(jnp.float32)
    core, gram = None, None
    for at in (2, 1, 0):
        stack = jnp.concatenate([tests] + parts[: 3 - at], axis=0)
        out = lax.dot_general(stack, parts[at], NT, preferred_element_type=jnp.float32)
        pieces = [out[size * p : size * (p + 1), :] for p in range(4 - at)]
        mirror = lax.dot_general(parts[at], tests, NT, preferred_element_type=jnp.float32)
        piece = pieces[0] + mirror
        core = piece if core is None else core + piece
        inner = pieces[-1]
        for piece in pieces[-2:0:-1]:
            inner = inner + piece
        gram = inner if gram is None else gram + inner
    return core * 0.5, (gram + gram.T) * 0.5


def again_kernel(first_ref, gram_ref):
    first = first_ref[...]
    _, gram = products(first.astype(jnp.bfloat16), first)
    gram_ref[...] = jnp.concatenate([gram, gram], axis=1)


def gram_kernel(members, near, *refs):
    totals, (tests_ref, gram_ref, sketched_ref, whole, tests) = refs[members - 1 :: -1], refs[members:]
    count = sketched_ref.shape[1]
    here = lax.axis_index("row") // 2 * near + lax.axis_index("col") % near
    for at in range(members):
        part = tree([
            totals[j][:, (at ^ j) * count : ((at ^ j) + 1) * count] for j in range(members)
        ])
        if at == 0:
            sketched_ref[...] = part
        place = pl.ds(pl.multiple_of((here ^ at) * count, count), count)
        whole[:, place] = part
        tests[:, place] = tests_ref[:, at * count : (at + 1) * count]
    core, gram = products(tests[...], whole[...])
    gram_ref[...] = jnp.concatenate([core, gram], axis=1)


def solve_kernel(scale, *refs):
    grams, (sketched_ref, basis_ref, first_ref, margin_ref) = refs[:-4], refs[-4:]
    both = tree([ref[...] for ref in grams[::-1]])
    size, rows = both.shape[0], 8
    count = size // rows
    sketched = sketched_ref[...]
    sides = [jnp.concatenate([sketched[:, at : at + size]] * 2, axis=1) for at in (0, size)]
    stacks = [[m[at : at + rows, :] for at in range(0, size, rows)] for m in [both] + sides]
    half = lax.broadcasted_iota(jnp.int32, (rows, 2 * size), 1) < size

    def spread(value):
        return jnp.broadcast_to(value, (rows, 2 * size))

    def column(value, at):
        left, right = value[:, at : at + 1], value[:, size + at : size + at + 1]
        return jnp.where(half, spread(left), spread(right))

    place = lax.broadcasted_iota(jnp.int32, (rows, 2 * size), 1)
    pivots = jnp.ones((rows, 2 * size), jnp.float32)
    outs = [[], []]
    for block in range(count):
        first_row = block * rows
        after = range(block + 1, count)
        columns = [column(stacks[0][block], first_row + j) for j in range(rows)]
        part = [[spread(columns[j][m : m + 1, :]) for j in range(m + 1)] for m in range(rows)]
        below = {b: [column(stacks[0][b], first_row + j) for j in range(rows)] for b in after}
        lines = [[spread(stack[block][j : j + 1, :]) for j in range(rows)] for stack in stacks]
        for j in range(rows):
            pivot = part[j][j]
            ahead = part[j + 1][j] * part[j + 1][j] if j + 1 < rows else None
            inverse = 1.0 / pivot
            pivots = jnp.where(place == size + first_row + j, pivot, pivots)
            for side, line in zip(outs, lines[1:]):
                side.append((line[j] * (lax.rsqrt(pivot) * scale))[:1, :])
            rest = range(j + 1, rows)
            factors = {m: part[m][j] * inverse for m in rest}
            for m in rest:
                for q in range(j + 1, m + 1):
                    lost = ahead * inverse if m == j + 1 else factors[m] * part[q][j]
                    part[m][q] = part[m][q] - lost
            for b in after:
                factor = below[b][j] * inverse
                for m in rest:
                    below[b][m] = below[b][m] - factor * part[m][j]
                for stack, line in zip(stacks, lines):
                    stack[b] = stack[b] - factor * line[j]
            for line in lines:
                for m in rest:
                    line[m] = line[m] - factors[m] * line[j]
    at_row = lax.broadcasted_iota(jnp.int32, both.shape, 0)
    at_lane = lax.broadcasted_iota(jnp.int32, both.shape, 1)
    diagonal = jnp.sum(jnp.where(at_lane == at_row + size, both, 0.0), axis=0, keepdims=True)
    kept = jnp.where(at_lane[:1] < size, 1.0, pivots[:1] / diagonal)
    margin_ref[0, 0] = (jnp.min(kept) > MARGIN).astype(jnp.int32)
    left, right = [jnp.concatenate(lines, axis=0) for lines in outs]
    first_ref[...] = jnp.concatenate([left[:, :size], right[:, :size]], axis=1)
    basis_ref[...] = jnp.concatenate([left[:, size:], right[:, size:]], axis=1)


def per_device(embeddings, sketch, rows, cols):
    count, width = embeddings.shape
    columns = sketch.shape[1]
    rate = 3.0 / width * LOG2E
    near = 2 if cols % 2 == 0 else 1
    members, others = rows // 2 * near, cols // near
    devices = rows * cols
    like = jax.ShapeDtypeStruct
    stay = pltpu.with_memory_space_constraint
    wide, chunk = members * count, 512

    def swap(value, mask):
        return lax.ppermute(value, AXES, [(i, i ^ mask) for i in range(devices)])

    def swaps(value, masks):
        return [swap(value, mask) for mask in masks]

    packed = pl.pallas_call(
        pack_kernel,
        out_shape=like((count + columns * count // width, width), embeddings.dtype),
        in_specs=[HBM, HBM],
        out_specs=VMEM,
        scratch_shapes=[pltpu.SemaphoreType.DMA((1 + width // count,))],
        compiler_params=params(4),
        name="pack",
    )(stay(embeddings, pltpu.HBM), stay(sketch.T, pltpu.HBM))
    own_masks = [2 * cols * x + l for x in range(rows // 2) for l in range(near)][1:]
    far_masks = [near * j for j in range(1, others)]
    facing = [packed] + swaps(packed, far_masks)
    own = [packed] + swaps(packed, own_masks)
    across = [swap(block, cols) for block in facing]
    early, late = facing + across[:1] + across[-1:], across[1:-1]

    def scratch(blocks):
        return [
            pltpu.VMEM((len(blocks) * count, width), embeddings.dtype),
            pltpu.VMEM((columns, len(blocks) * count), sketch.dtype),
        ]

    def cost(blocks):
        deep = len(blocks) * count
        return pl.CostEstimate(
            flops=2 * wide * deep * (width + columns),
            bytes_accessed=2 * (wide + deep) * width,
            transcendentals=wide * deep,
        )

    near_total, own_tests, own_points, weights = pl.pallas_call(
        functools.partial(near_kernel, members, chunk, rate),
        out_shape=(
            like((columns, wide), jnp.float32),
            like((columns, wide), sketch.dtype),
            like((wide, width), embeddings.dtype),
            like((8, wide), jnp.float32),
        ),
        in_specs=[VMEM] * (members + len(early) - 1),
        out_specs=(VMEM,) * 4,
        scratch_shapes=scratch(early),
        compiler_params=params(24),
        cost_estimate=cost(early),
        name="near",
    )(*own, *early[:0:-1])
    total = pl.pallas_call(
        functools.partial(far_kernel, chunk, rate),
        out_shape=like((columns, wide), jnp.float32),
        in_specs=[VMEM] * (3 + len(late)),
        out_specs=VMEM,
        scratch_shapes=scratch(late),
        compiler_params=params(24),
        cost_estimate=cost(late),
        name="far",
    )(near_total, own_points, weights, *late[::-1])
    totals = [total] + swaps(total, own_masks)
    gram, sketched = pl.pallas_call(
        functools.partial(gram_kernel, members, near),
        out_shape=(
            like((columns, 2 * columns), jnp.float32),
            like((columns, count), jnp.float32),
        ),
        in_specs=[VMEM] * (members + 1),
        out_specs=(VMEM, VMEM),
        scratch_shapes=[
            pltpu.VMEM((columns, wide), jnp.float32),
            pltpu.VMEM((columns, wide), sketch.dtype),
        ],
        compiler_params=params(24),
        name="gram",
    )(*totals[::-1], own_tests)
    gram = gram + swap(gram, cols)
    mask = near
    grams = [gram]
    while mask < cols:
        grams = [tree(grams)]
        masks = [mask, 2 * mask, 3 * mask] if 2 * mask < cols else [mask]
        grams += swaps(grams[0], masks)
        mask *= len(masks) + 1
    scale = float(devices * count) ** 0.5

    def solve(grams, sketched):
        return pl.pallas_call(
            functools.partial(solve_kernel, scale),
            out_shape=(
                like((columns, count), jnp.float32),
                like((columns, count), jnp.float32),
                pltpu.SMEM((1, 1), jnp.int32),
            ),
            in_specs=[VMEM] * (len(grams) + 1),
            out_specs=(VMEM, VMEM, pl.BlockSpec(memory_space=pltpu.SMEM)),
            compiler_params=params(8),
            name="solve",
        )(*grams, sketched)

    def refine(first, basis):
        gram = pl.pallas_call(
            again_kernel,
            out_shape=like((columns, 2 * columns), jnp.float32),
            in_specs=[VMEM],
            out_specs=VMEM,
            compiler_params=params(8),
            name="again",
        )(first)
        mask = 1
        while mask < devices:
            gram = gram + swap(gram, mask)
            mask *= 2
        return solve([gram], first)[0]

    basis, first, margin = solve(grams[::-1], sketched)
    basis = lax.switch(margin[0, 0], [refine, lambda first, basis: basis], first, basis)
    return basis.T, first.T


def solution(mesh):
    placed = P(AXES, None)
    return jax.shard_map(
        functools.partial(per_device, rows=mesh.shape["row"], cols=mesh.shape["col"]),
        mesh=mesh,
        in_specs=(placed, placed),
        out_specs=(placed, placed),
        check_vma=False,
    )
```
